32 devices in a mesh: res: 8 (over z, y), ch: 4 (over x, core).
Axes of the slice: x: 2, y: 2, z: 4, core: 2. Of those that a mesh axis runs over, the one named last changes fastest.
Arguments:
- sequence_matrix: bfloat16 [8, 512, 256], P(None, 'res'), may hold values from -6 to 6
- couple_matrix: bfloat16 [32, 128, 4096], P('res', 'ch')
- block_target_entry: int32 [8, 4], P('res'), may hold values from 0 to 7, as said below
- block_present_flag: int32 [8, 4], P('res'), may hold values from 0 to 1, as said below
- amino_strand: int32 [512], P('res'), may hold values from 0 to 5, never falling along the last dimension, each value on 1 to 170 neighbouring positions
- sequence_scaling_factor: float32 [256], replicated, may hold values from 0.5 to 1.5
- query_key_value_matrix: bfloat16 [4, 256, 256], P(None, None, 'ch'), may hold values from -0.375 to 0.375
- focus_result_matrix: bfloat16 [256, 256], P('ch'), may hold values from -0.375 to 0.375
- strand_focus_offset: float32 [8], replicated, may hold values from -2 to 2
- couple_scaling_factor: float32 [128], P('ch'), may hold values from 0.5 to 1.5
- focus_offset_matrix: float32 [128, 8], P('ch')
- product_scaling_factor: float32 [256], replicated, may hold values from 0.5 to 1.5
- first_factor_matrix: bfloat16 [256, 32], replicated, may hold values from -0.375 to 0.375
- second_factor_matrix: bfloat16 [256, 32], P(None, 'ch'), may hold values from -0.375 to 0.375
- product_result_matrix: bfloat16 [128, 32, 32], P(None, None, 'ch'), may hold values from -0.8984375 to 0.8984375
- product_result_offset: float32 [128], P('ch'), may hold values from -3 to 3
Outputs:
- sequence_result_matrix: bfloat16 [8, 512, 256], P(None, 'res')
- pairwise_output: bfloat16 [32, 128, 4096], P('res', 'ch')
The draws below stay inside these ranges and needn't reach their ends.
Inputs may be any that keep to these rules, and one draw needn't show every extreme that they name: `block_target_entry`: slot 0 of row tile r names r itself; the column tiles of one row tile are distinct. `block_present_flag`: the valid slots of each row tile are its first ones, two or more of them; in every draw some row tile has all 4 slots valid.
All inputs are finite; a program needn't handle non-finite values.
Results may differ from the reference program's by a relative error of at most 0.005.
Values may be sent and summed in bfloat16 or wider, within the bound.
No kernel may reach another device: no remote copies, remote signals or barrier semaphores. Data moves between devices by JAX's collectives and lax.ppermute only.
A program may use at most 128 MiB of HBM per device.

```python
import math
import jax
import jax.numpy as jnp
import numpy as np
from jax import lax

SEQUENCE_FEATURE = 256
C_Z = 128
FOCUS_NUMBER = 8
FOCUS_BREADTH = 32
PRODUCT_FEATURE = 32
TILE_RESIDUES = 64
SLOTS = 4
ROW_TILES = 8
AMINO_NUMBER = 512
SEQUENCE_NUMBER = 8


def channel_signs(key):
    flips = jax.random.randint(jax.random.fold_in(key, 71), (C_Z,), 0, 2)
    return (2 * flips - 1).astype(jnp.float32)


def tile_layout(key):
    base_key = jax.random.fold_in(key, 31)
    row_ids = jnp.arange(ROW_TILES, dtype=jnp.int32)
    ranks = jax.random.randint(jax.random.fold_in(base_key, 1), (ROW_TILES, ROW_TILES), 0, 1 << 16) * ROW_TILES + row_ids[None, :]
    diagonal = row_ids[:, None] == row_ids[None, :]
    ranks = jnp.where(diagonal, (1 << 16) * ROW_TILES + ROW_TILES, ranks)
    _, columns = lax.top_k(ranks, SLOTS)
    counts = jax.random.randint(jax.random.fold_in(base_key, 2), (ROW_TILES,), 2, SLOTS + 1)
    full_row = jax.random.randint(jax.random.fold_in(base_key, 3), (), 0, ROW_TILES)
    counts = jnp.where(row_ids == full_row, SLOTS, counts)
    usable = (jnp.arange(SLOTS, dtype=jnp.int32)[None, :] < counts[:, None]).astype(jnp.int32)
    return (columns.astype(jnp.int32), usable)


def draw_block_target_entry(key, part):
    return tile_layout(key)[0]


def draw_block_present_flag(key, part):
    return tile_layout(key)[1]


def draw_focus_offset_matrix(key, part):
    signs = channel_signs(key)
    magnitude = jax.random.uniform(jax.random.fold_in(key, 5), (C_Z,), jnp.float32, 0.5, 1.5)
    others = jax.random.normal(jax.random.fold_in(key, 6), (C_Z, FOCUS_NUMBER), jnp.float32)
    lead_scale = 0.15
    other_scale = 0.15
    weight = other_scale * others
    return weight.at[:, 0].set(lead_scale * signs * magnitude)


def draw_couple_matrix(key, part):
    tile_slots = ROW_TILES * SLOTS
    cell_count = TILE_RESIDUES * TILE_RESIDUES
    position = jnp.arange(C_Z, dtype=jnp.float32) / max(C_Z - 1, 1)
    rise = 3.0
    scale = jnp.power(rise, position) * jax.random.uniform(jax.random.fold_in(key, 12), (C_Z,), jnp.float32, 0.7, 1.4)
    noise = jnp.clip(jax.random.normal(jax.random.fold_in(key, 13), (tile_slots, C_Z, cell_count), jnp.float32), -4.0, 4.0)
    values = noise * scale[None, :, None]
    return values.astype(jnp.bfloat16)


def block_levels(own_key, extent, pieces, low, high):
    factor_of = 1.0
    for axis_at, shards_of in pieces:
        heights = jax.random.uniform(jax.random.fold_in(jax.random.fold_in(own_key, 6), axis_at), (shards_of,), jnp.float32, low / len(pieces), high / len(pieces))
        factor_of = factor_of * jnp.repeat(jnp.exp(heights), extent[axis_at] // shards_of).reshape((-1,) + (1,) * (len(extent) - 1 - axis_at))
    return factor_of


def split_up(count, total, limit, slope):
    portions = [(1 << 20) // math.isqrt(standing ** slope) + 1 for standing in range(2, count + 1)]
    surplus, given = total - limit - (count - 1), [1] * (count - 1)
    while surplus > 0:
        free = [i for i in range(count - 1) if given[i] < limit]
        pool, left = sum([portions[i] for i in free]), surplus
        for i in free:
            addition = min(limit - given[i], max(1, left * portions[i] // pool), surplus)
            given[i] = given[i] + addition
            surplus = surplus - addition
    return np.array([limit] + given)


def uneven(key, number_of, total, bound, skew):
    if number_of == 2:
        one = jax.random.randint(key, (), max(1, total - bound), min(bound, total - 1) + 1)
        return jnp.stack([one, total - one])
    lengths = jnp.asarray(split_up(number_of, total, bound, skew), jnp.int32)
    pairs = (number_of - 1) // 2
    donor, taker = lengths[1:1 + 2 * pairs:2], lengths[2:2 + 2 * pairs:2]
    room = jnp.minimum(donor - 1, bound - taker)
    shifted = jax.random.randint(jax.random.fold_in(key, 1), (pairs,), 0, 1 << 20) % (room + 1)
    lengths = lengths.at[1:1 + 2 * pairs:2].set(donor - shifted).at[2:2 + 2 * pairs:2].set(taker + shifted)
    return lengths[jax.random.permutation(jax.random.fold_in(key, 2), number_of)]


def centred(rng, shape, deviation, reach, pieces=(), kind=jnp.bfloat16):
    values = jax.random.normal(rng, shape, jnp.float32) * deviation
    if len(pieces) > 0:
        values = block_levels(rng, shape, pieces, -0.22, 0.18) * values
    return jnp.clip(values, min=-reach, max=reach).astype(kind)


def setup_inputs(seed: int = 0) -> dict:
    keys = jax.random.split(jax.random.key(seed), 17)
    return {
        "sequence_matrix": centred(keys[0], (SEQUENCE_NUMBER, AMINO_NUMBER, SEQUENCE_FEATURE), 1.0, 6.0, ((1, 8),)),
        "couple_matrix": draw_couple_matrix(jax.random.fold_in(keys[16], 71), 0),
        "block_target_entry": draw_block_target_entry(jax.random.fold_in(keys[16], 71), 0),
        "block_present_flag": draw_block_present_flag(jax.random.fold_in(keys[16], 71), 0),
        "amino_strand": jnp.searchsorted(jnp.cumsum(uneven(keys[4], 6, AMINO_NUMBER, AMINO_NUMBER // 3, 0)), jnp.arange(AMINO_NUMBER), side="right").astype(jnp.int32),
        "sequence_scaling_factor": jnp.clip(1.0 + 0.1 * jax.random.normal(keys[5], (SEQUENCE_FEATURE,), jnp.float32), 0.5, 1.5),
        "query_key_value_matrix": centred(keys[6], (4, SEQUENCE_FEATURE, FOCUS_NUMBER * FOCUS_BREADTH), SEQUENCE_FEATURE ** -0.5, 0.375, ((2, 4),)),
        "focus_result_matrix": centred(keys[7], (FOCUS_NUMBER * FOCUS_BREADTH, SEQUENCE_FEATURE), (FOCUS_NUMBER * FOCUS_BREADTH) ** -0.5, 0.375, ((0, 4),)),
        "strand_focus_offset": jnp.clip(jax.random.uniform(keys[8], (FOCUS_NUMBER,), jnp.float32, -2.0, 2.0), -2.0, 2.0),
        "couple_scaling_factor": jnp.clip(1.0 + 0.1 * jax.random.normal(keys[9], (C_Z,), jnp.float32), 0.5, 1.5),
        "focus_offset_matrix": draw_focus_offset_matrix(jax.random.fold_in(keys[16], 71), 0),
        "product_scaling_factor": jnp.clip(1.0 + 0.1 * jax.random.normal(keys[11], (SEQUENCE_FEATURE,), jnp.float32), 0.5, 1.5),
        "first_factor_matrix": centred(keys[12], (SEQUENCE_FEATURE, PRODUCT_FEATURE), SEQUENCE_FEATURE ** -0.5, 0.375),
        "second_factor_matrix": centred(keys[13], (SEQUENCE_FEATURE, PRODUCT_FEATURE), SEQUENCE_FEATURE ** -0.5, 0.375, ((1, 4),)),
        "product_result_matrix": centred(keys[14], (C_Z, PRODUCT_FEATURE, PRODUCT_FEATURE), 0.15, 0.8984375, ((2, 4),)),
        "product_result_offset": centred(keys[15], (C_Z,), 0.5, 3.0, ((0, 4),), jnp.float32),
    }


EPS = 1e-05
MASKED = -1e+30

def final_dimension_standardize(values, gain_vector):
    values = values.astype(jnp.float32)
    average = lax.optimization_barrier(jnp.mean(values, axis=-1, keepdims=True))
    variance = lax.optimization_barrier(jnp.mean(jnp.square(values - average), axis=-1, keepdims=True))
    return (values - average) * lax.rsqrt(variance + EPS) * gain_vector

def reference(sequence_matrix, couple_matrix, block_target_entry, block_present_flag, amino_strand, sequence_scaling_factor, query_key_value_matrix, focus_result_matrix, strand_focus_offset, couple_scaling_factor, focus_offset_matrix, product_scaling_factor, first_factor_matrix, second_factor_matrix, product_result_matrix, product_result_offset):
    sequence_number_here, amino_number_here, sequence_feature_breadth = sequence_matrix.shape
    tile_count = amino_number_here // TILE_RESIDUES
    inner_channels = FOCUS_NUMBER * FOCUS_BREADTH
    cell_count = TILE_RESIDUES * TILE_RESIDUES

    def tile_bias(tile_field):
        values = tile_field.astype(jnp.float32)
        average = lax.optimization_barrier(jnp.mean(values, axis=0, keepdims=True))
        variance = lax.optimization_barrier(jnp.mean(jnp.square(values - average), axis=0, keepdims=True))
        normed = (values - average) * lax.rsqrt(variance + EPS) * couple_scaling_factor[:, None]
        return jnp.dot(focus_offset_matrix.T, normed, precision=lax.Precision.HIGHEST).astype(jnp.bfloat16)
    pair_bias = lax.map(tile_bias, couple_matrix).reshape(tile_count, SLOTS, FOCUS_NUMBER, TILE_RESIDUES, TILE_RESIDUES)
    sequence_standardized = final_dimension_standardize(sequence_matrix, sequence_scaling_factor).astype(jnp.bfloat16).reshape(sequence_number_here * amino_number_here, sequence_feature_breadth)
    projected_rows = [jnp.dot(sequence_standardized, query_key_value_matrix[selected_slot], preferred_element_type=jnp.float32).astype(jnp.bfloat16).reshape(sequence_number_here, tile_count, TILE_RESIDUES, FOCUS_NUMBER, FOCUS_BREADTH) for selected_slot in range(4)]
    queries, keyset, valueset, gateset = projected_rows
    chain_tiles = amino_strand.reshape(tile_count, TILE_RESIDUES)

    def attend(tile_position):
        columns = block_target_entry[tile_position]
        usable = block_present_flag[tile_position] > 0
        query_tile = queries[:, tile_position].astype(jnp.float32)
        key_tiles = keyset[:, columns].astype(jnp.float32)
        value_tiles = valueset[:, columns].astype(jnp.float32)
        scores = jnp.einsum('rahd,rkbhd->rhakb', query_tile, key_tiles) * FOCUS_BREADTH ** (-0.5)
        same_chain = (chain_tiles[tile_position][:, None, None] == chain_tiles[columns][None, :, :]).astype(jnp.float32)
        extra = pair_bias[tile_position].astype(jnp.float32).transpose(1, 2, 0, 3)
        scores = scores + extra[None] + strand_focus_offset[None, :, None, None, None] * same_chain[None, None]
        scores = jnp.where(usable[None, None, None, :, None], scores, MASKED)
        row_max = lax.optimization_barrier(jnp.max(scores, axis=(3, 4), keepdims=True))
        exponent = jnp.exp(scores - row_max)
        attn_weights = (exponent / lax.optimization_barrier(jnp.sum(exponent, axis=(3, 4), keepdims=True))).astype(jnp.bfloat16)
        mixed = jnp.einsum('rhakb,rkbhd->rahd', attn_weights.astype(jnp.float32), value_tiles)
        gated = mixed * jax.nn.sigmoid(gateset[:, tile_position].astype(jnp.float32))
        return gated.astype(jnp.bfloat16)
    attended_rows = lax.map(attend, jnp.arange(tile_count, dtype=jnp.int32))
    attended_rows = attended_rows.transpose(1, 0, 2, 3, 4).reshape(sequence_number_here * amino_number_here, inner_channels)
    increment_change = jnp.dot(attended_rows, focus_result_matrix, preferred_element_type=jnp.float32)
    sequence_result_matrix = (sequence_matrix.astype(jnp.float32).reshape(sequence_number_here * amino_number_here, sequence_feature_breadth) + increment_change).astype(jnp.bfloat16).reshape(sequence_number_here, amino_number_here, sequence_feature_breadth)
    outer_normed = final_dimension_standardize(sequence_result_matrix, product_scaling_factor).astype(jnp.bfloat16).reshape(sequence_number_here * amino_number_here, sequence_feature_breadth)
    left_projected = jnp.dot(outer_normed, first_factor_matrix, preferred_element_type=jnp.float32).astype(jnp.bfloat16).reshape(sequence_number_here, amino_number_here, PRODUCT_FEATURE)
    right_projected = jnp.dot(outer_normed, second_factor_matrix, preferred_element_type=jnp.float32).astype(jnp.bfloat16).reshape(sequence_number_here, amino_number_here, PRODUCT_FEATURE)
    weight_flat = product_result_matrix.reshape(C_Z, PRODUCT_FEATURE * PRODUCT_FEATURE)

    def outer_tile(flat_index):
        tile_position = flat_index // SLOTS
        slot_index = flat_index % SLOTS
        column_index = block_target_entry[tile_position, slot_index]
        left_tile_rows = lax.dynamic_slice_in_dim(left_projected, (tile_position * TILE_RESIDUES).astype(jnp.int32), TILE_RESIDUES, 1).reshape(sequence_number_here, TILE_RESIDUES * PRODUCT_FEATURE)
        right_tile_rows = lax.dynamic_slice_in_dim(right_projected, (column_index * TILE_RESIDUES).astype(jnp.int32), TILE_RESIDUES, 1).reshape(sequence_number_here, TILE_RESIDUES * PRODUCT_FEATURE)
        outer_mean = jnp.dot(left_tile_rows.T, right_tile_rows, preferred_element_type=jnp.float32) / sequence_number_here
        outer_mean = outer_mean.reshape(TILE_RESIDUES, PRODUCT_FEATURE, TILE_RESIDUES, PRODUCT_FEATURE).transpose(1, 3, 0, 2).astype(jnp.bfloat16).reshape(PRODUCT_FEATURE * PRODUCT_FEATURE, cell_count)
        update = jnp.dot(weight_flat, outer_mean, preferred_element_type=jnp.float32) + product_result_offset[:, None]
        keep_mask = block_present_flag[tile_position, slot_index].astype(jnp.float32)
        return (couple_matrix[flat_index].astype(jnp.float32) + keep_mask * update).astype(jnp.bfloat16)
    pairwise_output = lax.map(outer_tile, jnp.arange(tile_count * SLOTS, dtype=jnp.int32))
    return (sequence_result_matrix, pairwise_output)
```

```python
import functools
import math

import jax
import jax.numpy as jnp
from jax import lax
from jax.experimental import pallas as pl
from jax.experimental.pallas import tpu as pltpu
from jax.sharding import PartitionSpec as P


C_Z = 128
FOCUS_NUMBER = 8
FOCUS_BREADTH = 32
PRODUCT_FEATURE = 32


EPS = 1e-05
MASKED = -1e30


def final_dimension_standardize(values, gain_vector):
    values = values.astype(jnp.float32)
    average = jnp.mean(values, axis=-1, keepdims=True)
    variance = jnp.mean(jnp.square(values - average), axis=-1, keepdims=True)
    return (values - average) * lax.rsqrt(variance + EPS) * gain_vector


def on_device(
    sequence_matrix,
    couple_matrix,
    block_target_entry,
    block_present_flag,
    amino_strand,
    sequence_scaling_factor,
    query_key_value_matrix,
    focus_result_matrix,
    strand_focus_offset,
    couple_scaling_factor,
    focus_offset_matrix,
    product_scaling_factor,
    first_factor_matrix,
    second_factor_matrix,
    product_result_matrix,
    product_result_offset,
):
    groups = lax.axis_size("ch")
    group_index = lax.axis_index("ch")
    local_heads = FOCUS_NUMBER // groups
    slot_count = couple_matrix.shape[0]
    cell_count = couple_matrix.shape[2]
    block_extent = sequence_matrix.shape[1]
    sequence_number_overall = sequence_matrix.shape[0]
    pair_field = couple_matrix.astype(jnp.float32)
    part_one = jnp.sum(pair_field, axis=1)
    part_two = jnp.sum(pair_field * pair_field, axis=1)
    sum_one, sum_two = lax.psum((part_one, part_two), "ch")
    center = sum_one / C_Z
    spread = lax.rsqrt(sum_two / C_Z - center * center + EPS)
    normed = (
        (pair_field - center[:, None, :])
        * spread[:, None, :]
        * couple_scaling_factor[None, :, None]
    )
    partial_value = jnp.einsum(
        "kcp,ch->hkp", normed, focus_offset_matrix, precision=lax.Precision.HIGHEST
    )
    head_bias = lax.psum_scatter(partial_value, "ch", scatter_dimension=0, tiled=True)
    head_bias = head_bias.astype(jnp.bfloat16)
    bias_all, cols_all, valid_all, chain_all = (
        lax.all_gather(head_bias, "res", axis=1, tiled=True),
        lax.all_gather(block_target_entry, "res", axis=0, tiled=True),
        lax.all_gather(block_present_flag, "res", axis=0, tiled=True),
        lax.all_gather(amino_strand, "res", axis=0, tiled=True),
    )
    sequence_first_layout = lax.all_to_all(
        sequence_matrix, "res", split_axis=0, concat_axis=1, tiled=True
    )
    device_rows, amino_number_here, sequence_feature_breadth = sequence_first_layout.shape
    tile_count = amino_number_here // block_extent
    sequence_standardized = final_dimension_standardize(
        sequence_first_layout, sequence_scaling_factor
    ).astype(jnp.bfloat16)
    projected_rows = jnp.einsum(
        "hbx,sxt->shbt",
        sequence_standardized,
        query_key_value_matrix,
        preferred_element_type=jnp.float32,
    ).astype(jnp.bfloat16)
    projected_rows = projected_rows.reshape(
        4, device_rows, tile_count, block_extent, local_heads, FOCUS_BREADTH
    )
    queries = projected_rows[0]
    keyset = projected_rows[1]
    valueset = projected_rows[2]
    gateset = projected_rows[3]
    chain_tiles = chain_all.reshape(tile_count, block_extent)
    bias_tiles = bias_all.reshape(local_heads, tile_count, slot_count, block_extent, block_extent)
    head_scale = lax.dynamic_slice_in_dim(
        strand_focus_offset, group_index * local_heads, local_heads, 0
    )
    block_tiles = math.gcd(tile_count, max(1, 512 // block_extent))

    def attend(block_index):
        first_tile = block_index * block_tiles
        columns = lax.dynamic_slice_in_dim(cols_all, first_tile, block_tiles, 0)
        usable = lax.dynamic_slice_in_dim(valid_all, first_tile, block_tiles, 0) > 0
        query_block = lax.dynamic_slice_in_dim(queries, first_tile, block_tiles, 1)
        key_block = keyset[:, columns]
        value_block = valueset[:, columns]
        scores = jnp.einsum(
            "rgahd,rgkbhd->rghakb", query_block, key_block, preferred_element_type=jnp.float32
        ) * FOCUS_BREADTH ** (-0.5)
        pair_part = lax.dynamic_slice_in_dim(bias_tiles, first_tile, block_tiles, 1).astype(
            jnp.float32
        )
        pair_part = pair_part.transpose(1, 0, 3, 2, 4)
        query_chain = lax.dynamic_slice_in_dim(chain_tiles, first_tile, block_tiles, 0)
        same_chain = (query_chain[:, :, None, None] == chain_tiles[columns][:, None, :, :]).astype(
            jnp.float32
        )
        scores = (
            scores
            + pair_part[None]
            + head_scale[None, None, :, None, None, None] * same_chain[None, :, None]
        )
        scores = jnp.where(usable[None, :, None, None, :, None], scores, MASKED)
        row_max = jnp.max(scores, axis=(4, 5), keepdims=True)
        exponent = jnp.exp(scores - row_max)
        attn_weights = (exponent / jnp.sum(exponent, axis=(4, 5), keepdims=True)).astype(
            jnp.bfloat16
        )
        mixed = jnp.einsum(
            "rghakb,rgkbhd->rgahd", attn_weights, value_block, preferred_element_type=jnp.float32
        )
        gate_block = lax.dynamic_slice_in_dim(gateset, first_tile, block_tiles, 1).astype(
            jnp.float32
        )
        return (mixed * jax.nn.sigmoid(gate_block)).astype(jnp.bfloat16)

    blocks = lax.map(attend, jnp.arange(tile_count // block_tiles, dtype=jnp.int32))
    attended_rows = blocks.transpose(1, 0, 2, 3, 4, 5).reshape(
        device_rows * amino_number_here, local_heads * FOCUS_BREADTH
    )
    residual_input = sequence_first_layout.reshape(
        device_rows * amino_number_here, sequence_feature_breadth
    )
    partial_out = jnp.dot(attended_rows, focus_result_matrix, preferred_element_type=jnp.float32)
    head_total = lax.psum(partial_out, "ch")
    updated_state = (
        (residual_input.astype(jnp.float32) + head_total)
        .astype(jnp.bfloat16)
        .reshape(device_rows, amino_number_here, sequence_feature_breadth)
    )
    sequence_result_matrix = lax.all_to_all(
        updated_state, "res", split_axis=1, concat_axis=0, tiled=True
    )
    outer_normed = (
        final_dimension_standardize(sequence_result_matrix, product_scaling_factor)
        .astype(jnp.bfloat16)
        .reshape(sequence_number_overall * block_extent, sequence_feature_breadth)
    )
    left_projected = (
        jnp.dot(outer_normed, first_factor_matrix, preferred_element_type=jnp.float32)
        .astype(jnp.bfloat16)
        .reshape(sequence_number_overall, block_extent * PRODUCT_FEATURE)
    )
    own_columns = block_target_entry[0]
    right_projected = (
        jnp.dot(outer_normed, second_factor_matrix, preferred_element_type=jnp.float32)
        .astype(jnp.bfloat16)
        .reshape(sequence_number_overall, block_extent, -1)
    )
    narrow = right_projected.shape[2]
    weight_flat = product_result_matrix.reshape(C_Z, PRODUCT_FEATURE * narrow)
    empty_tiles = jnp.zeros(
        (slot_count, sequence_number_overall, block_extent, narrow), jnp.bfloat16
    )
    shard_piece = lax.all_gather(right_projected, "res", axis=1, tiled=True)
    piece_rows = shard_piece.shape[1]
    offset = own_columns * block_extent
    inside = (offset >= 0) & (offset < piece_rows)

    def take_one(offset_one, inside_one, held_tile):
        taken = lax.dynamic_slice_in_dim(
            shard_piece, jnp.clip(offset_one, 0, piece_rows - block_extent), block_extent, 1
        )
        return jnp.where(inside_one, taken, held_tile)

    chosen = jax.vmap(take_one, in_axes=(0, 0, 0))(offset, inside, empty_tiles)
    left_turned = left_projected.T

    def outer_one(right_tile_rows):
        product = (
            jnp.dot(
                left_turned,
                right_tile_rows.reshape(sequence_number_overall, block_extent * narrow),
                preferred_element_type=jnp.float32,
            )
            / sequence_number_overall
        )
        product = (
            product.reshape(block_extent, PRODUCT_FEATURE, block_extent, narrow)
            .transpose(1, 3, 0, 2)
            .astype(jnp.bfloat16)
            .reshape(PRODUCT_FEATURE * narrow, cell_count)
        )
        return jnp.dot(weight_flat, product, preferred_element_type=jnp.float32)

    partials = lax.map(outer_one, chosen)
    summed = lax.psum_scatter(partials, "ch", scatter_dimension=1, tiled=True)
    keep_mask = block_present_flag[0].astype(jnp.float32)
    pairwise_output = (
        pair_field + keep_mask[:, None, None] * (summed + product_result_offset[None, :, None])
    ).astype(jnp.bfloat16)
    return (sequence_result_matrix, pairwise_output)


ACROSS = (((1,), (0,)), ((), ()))
BOTH_LAST = (((1,), (1,)), ((), ()))
VMEM_LIMIT = 12 * 1024 * 1024


def flip(values, axis, bits):
    size = lax.axis_size(axis)
    return lax.ppermute(values, axis, [(i, i ^ bits) for i in range(size)])


def over_groups(values, relay):
    across = flip(values, "ch", 2)
    near = flip(values, "ch", 1)
    if relay:
        far = flip(across, "ch", 1)
    else:
        far = flip(values, "ch", 3)
    return [values, near, across, far]


def over_tiles(values):
    size = lax.axis_size("res")
    found = {0: values}
    for bits in range(size - 2, 0, -2):
        found[bits] = flip(values, "res", bits)
    for bits in range(0, size, 2):
        found[bits + 1] = flip(found[bits], "res", 1)
    return [found[bits] for bits in range(size)]


def dot(a, b, dims):
    return lax.dot_general(a, b, dims, preferred_element_type=jnp.float32)


def lane_block(shape, width):
    return lax.broadcasted_iota(jnp.int32, shape, len(shape) - 1) // width


def standardized(values, gain):
    average = jnp.mean(values, axis=-1, keepdims=True)
    centred = values - average
    variance = jnp.mean(centred * centred, axis=-1, keepdims=True)
    return centred * lax.rsqrt(variance + EPS) * gain


def put(ref, values):
    for b in range(ref.shape[0]):
        ref[b] = values[:, b * 128 : (b + 1) * 128]


def take(ref):
    return jnp.concatenate([ref[b] for b in range(ref.shape[0])], axis=1)


def put_every(ref, start, step, values, first=0):
    for b in range(values.shape[1] // 128):
        ref[first + b, pl.ds(start, values.shape[0], stride=step), :] = values[
            :, b * 128 : (b + 1) * 128
        ]


def take_every(ref, start, size, step):
    return jnp.concatenate(
        [ref[b, pl.ds(start, size, stride=step), :] for b in range(ref.shape[0])], axis=1
    )


def spec():
    return pl.BlockSpec(memory_space=pltpu.VMEM)


def call(body, out, inputs, specs, scratch, flops, moved):
    out_specs = jax.tree.map(lambda _: spec(), out)
    return pl.pallas_call(
        body,
        out_shape=out,
        in_specs=specs,
        out_specs=out_specs,
        scratch_shapes=scratch,
        cost_estimate=pl.CostEstimate(flops=flops, bytes_accessed=moved, transcendentals=0),
        compiler_params=pltpu.CompilerParams(vmem_limit_bytes=VMEM_LIMIT),
    )(*inputs)


def column(row, lanes):
    return jnp.broadcast_to(row, (lanes, row.shape[1])).T


def prepare(extent, rows, *refs):
    sources, outs, scratch = refs[:16], refs[16:28], refs[28:]
    sequence, pair, query_key_value, out_weight, second, strand = sources[:6]
    gain_pair, focus, gain_one, gain_two, first, offset, chain_gain = sources[6:13]
    product, target, present = sources[13:]
    tile_ref, weight_ref, pair_ref, sum_weight_ref, gain_one_ref, gain_two_ref = outs[:6]
    first_ref, offset_ref, chain_ref, chain_gain_ref, place_ref, open_ref = outs[6:]
    held_second, held_strand, held_gain, held_focus, held_first, held_offset = scratch[:6]
    held_chain_gain, held_target, held_present, wide, tall, sems = scratch[6:]
    lines = rows * extent
    group = lax.axis_index("ch")
    narrow = second.shape[0]
    moves = [
        (strand, held_strand),
        (second, held_second),
        (gain_pair, held_gain),
        (focus, held_focus),
        (first, held_first),
        (offset, held_offset),
        (chain_gain, held_chain_gain),
        (target, held_target),
        (present, held_present),
        (gain_one, gain_one_ref),
        (gain_two, gain_two_ref),
        (out_weight, weight_ref.at[4]),
        (query_key_value, weight_ref.at[0:4]),
        (pair, pair_ref),
    ]
    deep = weight_ref.shape[1]
    for i in range(product.shape[0] // deep):
        part = pl.ds((i % 2) * 128, 128)
        moves.append(
            (product.at[pl.ds(i * deep, deep)], weight_ref.at[6 + i // 2, :, part])
        )
    for s in range(rows):
        moves.append(
            (sequence.at[group * rows + s], tile_ref.at[s * extent : (s + 1) * extent])
        )
    copies = [
        pltpu.make_async_copy(source, target, sems.at[i])
        for i, (source, target) in enumerate(moves)
    ]
    for copy in copies:
        copy.start()
    for copy in copies[:9]:
        copy.wait()
    width = tile_ref.shape[1]
    tile = lax.axis_index("res")
    slots = target.shape[1]
    for k in range(slots):
        place_ref[k : k + 1, :] = jnp.full((1, 128), held_target[0, k] ^ tile)
        open_ref[k : k + 1, :] = jnp.full((1, 128), held_present[0, k]).astype(jnp.float32)
    chain = held_strand[...].astype(jnp.float32)
    twice = jnp.concatenate([chain] * (128 // extent), axis=1)
    line = jnp.broadcast_to(jnp.concatenate([twice] * (width // 128), axis=1), (8, width))
    tile_ref[lines:, :] = line.astype(jnp.bfloat16)
    tall[...] = column(chain, 128)
    half = extent // 2
    for p in range(2):
        chain_ref[p * half : (p + 1) * half, :] = tall[pl.ds(p, half, stride=2), :]
    spread = lax.broadcasted_iota(jnp.int32, (weight_ref.shape[1], width), 0)
    factor = jnp.concatenate(
        [held_second[...].astype(jnp.float32)] * (weight_ref.shape[1] // narrow), axis=0
    )
    weight_ref[5] = jnp.where(spread // narrow == group, factor, 0.0).astype(jnp.bfloat16)
    gains = held_focus[...] * held_gain[...]
    one = gains.astype(jnp.bfloat16).astype(jnp.float32)
    two = (gains - one).astype(jnp.bfloat16).astype(jnp.float32)
    sum_weight_ref[...] = jnp.concatenate(
        [one, two, gains - one - two, jnp.ones_like(gains)], axis=0
    ).astype(jnp.bfloat16)
    put(wide, held_first[...].astype(jnp.float32))
    features = first_ref.shape[0]
    first_ref[...] = jnp.concatenate(
        [take_every(wide, i, features // 4, 4) for i in range(4)], axis=0
    ).astype(jnp.bfloat16)
    offset_ref[...] = column(held_offset[...], 128)
    chain_gain_ref[...] = column(held_chain_gain[...], 128)
    for copy in copies[9:]:
        copy.wait()


def pair_sums(keep, weight_ref, pair_ref, out_ref):
    slots = pair_ref.shape[0] // 2
    channels, cells = pair_ref.shape[1:]
    odd = lax.rem(lax.axis_index("ch"), 2)
    half = odd if keep else 1 - odd
    weights = weight_ref[...]
    heads = FOCUS_NUMBER
    pieces = heads // 2
    stretch = cells // pieces
    total = jnp.sum(weights.astype(jnp.float32), axis=1, keepdims=True)
    gain = total[0:heads] + total[heads : 2 * heads] + total[2 * heads : 3 * heads]
    step = 512
    for k in range(slots):
        slot = half * slots + k
        for start in range(0, cells, step):
            part = pl.ds(start, step)
            block = pair_ref[slot, :, part]
            sums = dot(weights, block, ACROSS)
            mean = sums[3 * heads : 3 * heads + 1] * (1.0 / channels)
            head = sums[0:heads] + sums[heads : 2 * heads] + sums[2 * heads : 3 * heads]
            centred = block.astype(jnp.float32) - mean
            out_ref[k, :, part] = head - mean * gain
            piece = start // stretch
            line = pl.ds(cells + start % stretch, step)
            out_ref[k, piece : piece + 1, line] = mean
            out_ref[k, pieces + piece : pieces + piece + 1, line] = jnp.sum(
                centred * centred, axis=0, keepdims=True
            )
        out_ref[k, :, cells + stretch :] = jnp.broadcast_to(gain, (heads, 128))


def merge_sums(count, own_ref, other_ref, kept_ref, sent_ref):
    heads, width = kept_ref.shape
    pieces = heads // 2
    stretch = (width - 128) // (pieces + 1)
    cells = pieces * stretch
    high = lax.axis_index("ch") // 2
    step = 512
    for slot, out_ref in ((high, kept_ref), (1 - high, sent_ref)):
        gain_own = own_ref[slot, :, cells + stretch :]
        gain_other = other_ref[slot, :, cells + stretch :]
        half_gain = 0.5 * (gain_own - gain_other)[:, 0:1]
        out_ref[:, cells + stretch :] = gain_own + gain_other
        for start in range(cells, cells + stretch, step):
            part = pl.ds(start, step)
            own = own_ref[slot, :, part]
            other = other_ref[slot, :, part]
            apart = (own - other)[0:pieces]
            both = own + other
            out_ref[:, part] = jnp.concatenate(
                [0.5 * both[0:pieces], both[pieces:] + apart * apart * (0.5 * count)], axis=0
            )
        for start in range(0, cells, step):
            part = pl.ds(start, step)
            piece = start // stretch
            line = pl.ds(cells + start % stretch, step)
            apart = (
                own_ref[slot, piece : piece + 1, line] - other_ref[slot, piece : piece + 1, line]
            )
            out_ref[:, part] = own_ref[slot, :, part] + other_ref[slot, :, part] + apart * half_gain


def pair_bias(extent, own_ref, far_ref, out_ref, lines):
    heads, width = own_ref.shape
    half = extent // 2
    pieces = heads // 2
    stretch = (width - 128) // (pieces + 1)
    cells = pieces * stretch
    gain = own_ref[:, cells + stretch :] - far_ref[:, cells + stretch :]
    half_gain = 0.5 * gain[:, 0:1]
    step = 512
    for start in range(0, cells, step):
        part = pl.ds(start, step)
        piece = start // stretch
        line = pl.ds(cells + start % stretch, step)
        mean = slice(piece, piece + 1)
        square = slice(pieces + piece, pieces + piece + 1)
        apart = own_ref[mean, line] - far_ref[mean, line]
        spread = own_ref[square, line] + far_ref[square, line] + apart * apart * (C_Z / 4.0)
        inverse = lax.rsqrt(spread * (1.0 / C_Z) + EPS)
        head = (own_ref[:, part] + far_ref[:, part] + apart * half_gain) * inverse
        for inner in range(step // 128):
            lines[pl.ds(start // 128 + inner, heads, stride=half), :] = head[
                :, inner * 128 : (inner + 1) * 128
            ]
    out_ref[...] = lines[...].astype(jnp.bfloat16)


def project(extent, rows, tiles, place_ref, *refs):
    tile_refs, weight_refs = refs[:tiles], refs[tiles : tiles + 4]
    gain_ref = refs[tiles + 4]
    key_ref, value_ref, query_ref, gate_ref, chain_ref, stack = refs[tiles + 5 :]
    lines = rows * extent
    slots = chain_ref.shape[0]
    for m in range(tiles):
        stack[m] = tile_refs[m][...]
    gain = gain_ref[...]
    weights = [
        jnp.concatenate([ref[kind] for ref in weight_refs], axis=0) for kind in range(4)
    ]
    for k in range(slots):
        place = place_ref[k, 0]
        tile = stack[place, 0:lines, :].astype(jnp.float32)
        chain_ref[k] = stack[place, lines : lines + 8, 0:128].astype(jnp.float32)
        normed = standardized(tile, gain).astype(jnp.bfloat16)
        if k == 0:
            put(query_ref, dot(normed, weights[0], BOTH_LAST).astype(jnp.bfloat16).astype(jnp.float32))
            gate_ref[...] = dot(normed, weights[3], BOTH_LAST).astype(jnp.bfloat16)
        keys = dot(normed, weights[1], BOTH_LAST).astype(jnp.bfloat16)
        values = dot(normed, weights[2], BOTH_LAST).astype(jnp.bfloat16)
        for s in range(rows):
            part = slice(s * extent, (s + 1) * extent)
            key_ref[s, k * extent : (k + 1) * extent, :] = keys[part]
            value_ref[s, k * extent : (k + 1) * extent, :] = values[part]


def attention(extent, rows, *refs):
    key_ref, value_ref, query_ref, gate_ref, key_chain_ref, tile_ref = refs[:6]
    weight_refs = refs[6:10]
    bias_refs = refs[10:14]
    chain_ref, chain_gain_ref, gain_ref, open_ref = refs[14:18]
    row_ref, right_ref, pair, bias, attended = refs[18:]
    slots = key_chain_ref.shape[0]
    heads = FOCUS_NUMBER
    local_heads = heads // 4
    width = row_ref.shape[1]
    half = extent // 2
    lines = rows * extent
    group = lax.axis_index("ch")
    for m in range(4):
        other = group ^ m
        pair[2 * lax.rem(other, 2) + other // 2] = bias_refs[m][...]

    low = lax.broadcasted_iota(jnp.int32, (half, 128), 1) < extent
    for k in range(0, slots, 2):
        chain = jnp.where(low[0:1], key_chain_ref[k, 0:1], key_chain_ref[k + 1, 0:1])
        is_open = jnp.where(low, open_ref[k : k + 1, :], open_ref[k + 1 : k + 2, :]) > 0.0
        same = [
            (chain_ref[p * half : (p + 1) * half, :] == chain).astype(jnp.float32)
            for p in range(2)
        ]
        lanes = slice((k // 2) * 128, (k // 2 + 1) * 128)
        for h in range(heads):
            rows_h = slice(h * half, (h + 1) * half)
            zero = pair[k, rows_h, :].astype(jnp.float32)
            one = pair[k + 1, rows_h, :].astype(jnp.float32)
            joined = (
                jnp.where(low, zero, pltpu.roll(one, extent, 1)),
                jnp.where(low, pltpu.roll(zero, extent, 1), one),
            )
            for p in range(2):
                value = joined[p] + chain_gain_ref[h : h + 1, :] * same[p]
                bias[p, rows_h, lanes] = jnp.where(is_open, value, MASKED)

    head_lane = lane_block((half, width), FOCUS_BREADTH)
    for s in range(rows):
        for p in range(2):
            asked = take_every(query_ref, s * extent + p, half, 2)
            asked = jnp.concatenate(
                [jnp.where(head_lane == h, asked, 0.0) for h in range(heads)], axis=0
            ).astype(jnp.bfloat16)
            scores = dot(asked, key_ref[s], BOTH_LAST) * FOCUS_BREADTH ** (-0.5)
            parts = []
            for h in range(heads):
                index = (group ^ (h // local_heads)) * local_heads + h % local_heads
                start = pl.multiple_of(index * half, half)
                parts.append(
                    scores[h * half : (h + 1) * half] + bias[p, pl.ds(start, half), :]
                )
            scores = jnp.concatenate(parts, axis=0)
            peak = jnp.max(scores, axis=1, keepdims=True)
            exponent = jnp.exp(scores - peak)
            share = 1.0 / jnp.sum(exponent, axis=1, keepdims=True)
            weight = (exponent * share).astype(jnp.bfloat16)
            mixed = dot(weight, value_ref[s], ACROSS)
            kept = jnp.zeros((half, width), jnp.float32)
            for h in range(heads):
                kept = kept + jnp.where(head_lane == h, mixed[h * half : (h + 1) * half], 0.0)
            put_every(attended, s * extent + p, 2, kept)
    gates = gate_ref[...].astype(jnp.float32)
    gated = (take(attended) * jax.nn.sigmoid(gates)).astype(jnp.bfloat16)
    out_weight = jnp.concatenate([ref[4] for ref in weight_refs], axis=0)
    change = dot(gated, out_weight, ACROSS)
    updated = (tile_ref[0:lines, :].astype(jnp.float32) + change).astype(jnp.bfloat16)
    row_ref[...] = updated
    opm = standardized(updated.astype(jnp.float32), gain_ref[...]).astype(jnp.bfloat16)
    factor = weight_refs[0][5].astype(jnp.float32)
    for ref in weight_refs[1:]:
        factor = factor + ref[5].astype(jnp.float32)
    factor = factor[0:PRODUCT_FEATURE].astype(jnp.bfloat16)
    right_ref[...] = dot(factor, opm, BOTH_LAST).astype(jnp.bfloat16)


def product_tables(*refs):
    piece_refs = refs[:4]
    table_ref, stack, turned, lined = refs[4:]
    features, narrow, channels = stack.shape[1:]
    share = channels // 4
    group = lax.axis_index("ch")
    deep = piece_refs[0].shape[1]
    for m in range(4):
        for i in range(features * narrow // deep):
            part = piece_refs[m][6 + i // 2, :, (i % 2) * 128 : (i % 2 + 1) * 128]
            few = deep // narrow
            stack[group ^ m, i * few : (i + 1) * few] = part.astype(
                jnp.float32
            ).reshape(few, narrow, channels)
    own = pl.multiple_of(group * share, share)
    lines = features // 4
    for block in range(lines):
        tall = jnp.concatenate(
            [
                stack[m, block * 4 + i]
                for i in range(4)
                for m in range(4)
            ],
            axis=0,
        )
        turned[...] = tall.T
        lined[pl.ds(block, share, stride=lines), :] = turned[pl.ds(own, share), :]
    lanes = lane_block((lines, 128), features)
    for z in range(share):
        rows = lined[z * lines : (z + 1) * lines, :]
        moved = [rows] + [pltpu.roll(rows, by * features, 1) for by in range(1, 4)]
        parts = [
            jnp.where(lanes == s, moved[(s - i) % 4], 0.0) for s in range(4) for i in range(4)
        ]
        table_ref[z // 2, :, (z % 2) * 128 : (z % 2 + 1) * 128] = jnp.concatenate(
            parts, axis=0
        ).astype(jnp.bfloat16)


def left_tables(extent, rows, *refs):
    piece_refs = refs[:4]
    factor_ref, gain_ref, weight_ref = refs[4:7]
    table_ref, result_ref = refs[7:9]
    spread, natural = refs[9:]
    half = extent // 2
    features = PRODUCT_FEATURE
    lines = rows * extent
    factor = jnp.concatenate([factor_ref[...]] * 4, axis=0)
    lanes = lane_block((lines, 128), features)
    left = jnp.zeros((lines, 128), jnp.float32)
    for m in range(4):
        piece = piece_refs[m][...]
        group = lax.axis_index("ch") ^ m
        for s in range(rows):
            result_ref[group * rows + s] = piece[s * extent : (s + 1) * extent]
        normed = standardized(piece.astype(jnp.float32), gain_ref[...]).astype(jnp.bfloat16)
        left = left + jnp.where(lanes == m, dot(normed, factor, BOTH_LAST), 0.0)
    natural[...] = left
    left = jnp.concatenate(
        [
            natural[pl.ds(s * extent + p, half, stride=2), :]
            for p in range(2)
            for s in range(rows)
        ],
        axis=0,
    ).astype(jnp.bfloat16)
    pairs = weight_ref.shape[0]
    for z in range(pairs):
        table = dot(left, weight_ref[z], ACROSS)
        for b in range(2 * rows):
            for q in range(2):
                spread[b, pl.ds(2 * z + q, half, stride=2 * pairs), :] = table[
                    b * half : (b + 1) * half, q * 128 : (q + 1) * 128
                ]
    for b in range(2 * rows):
        table_ref[:, b * 128 : (b + 1) * 128] = spread[b].astype(jnp.bfloat16)


def pick(place_ref, even_ref, odd_ref, out_ref):
    for k in range(out_ref.shape[0]):
        place = place_ref[k, 0]
        even = even_ref[place // 2]
        odd = odd_ref[place // 2]
        out_ref[k] = jnp.where(lax.rem(place, 2) == 0, even, odd)


def pair_update(extent, rows, scale, open_ref, table_ref, pair_ref, offset_ref, *refs):
    piece_refs = refs[:4]
    out_ref, right, held, sems = refs[4:]
    slots, channels, cells = pair_ref.shape
    low = lax.broadcasted_iota(jnp.int32, (4 * piece_refs[0].shape[1], 128), 1) < extent
    for k in range(slots):
        one = jnp.concatenate([ref[k] for ref in piece_refs], axis=0).astype(jnp.float32)
        turned = pltpu.roll(one, extent, 1)
        depth = one.shape[0]
        for p in range(2):
            for s in range(rows):
                value = one if s == p else turned
                value = jnp.where(low if p == 0 else jnp.logical_not(low), value, 0.0)
                start = (p * rows + s) * depth
                right[start : start + depth, k * 128 : (k + 1) * 128] = value.astype(
                    jnp.bfloat16
                )
    offset = offset_ref[...]
    keep = [open_ref[k : k + 1, :] for k in range(slots)]
    steps = sems.shape[0]
    stretch = cells // steps
    deep = stretch // 128
    copies = []
    for i in range(steps):
        total = dot(
            table_ref[i * deep * channels : (i + 1) * deep * channels, :], right[...], ACROSS
        )
        for k in range(slots):
            for line in range(deep):
                update = total[line * channels : (line + 1) * channels, k * 128 : (k + 1) * 128]
                update = update * scale + offset
                cell = slice((i * deep + line) * 128, (i * deep + line + 1) * 128)
                held[k, :, cell] = (
                    pair_ref[k, :, cell].astype(jnp.float32) + keep[k] * update
                ).astype(jnp.bfloat16)
        part = pl.ds(i * stretch, stretch)
        copies.append(
            pltpu.make_async_copy(held.at[:, :, part], out_ref.at[:, :, part], sems.at[i])
        )
        copies[-1].start()
    for copy in copies:
        copy.wait()


def on_device_small(*arguments):
    return small(*arguments)


def small(
    sequence_matrix,
    couple_matrix,
    block_target_entry,
    block_present_flag,
    amino_strand,
    sequence_scaling_factor,
    query_key_value_matrix,
    focus_result_matrix,
    strand_focus_offset,
    couple_scaling_factor,
    focus_offset_matrix,
    product_scaling_factor,
    first_factor_matrix,
    second_factor_matrix,
    product_result_matrix,
    product_result_offset,
):
    groups = lax.axis_size("ch")
    tiles = lax.axis_size("res")
    sequences, extent, width = sequence_matrix.shape
    slots, channels, cells = couple_matrix.shape
    rows = sequences // groups
    lines = rows * extent
    heads = FOCUS_NUMBER
    features = PRODUCT_FEATURE
    half = extent // 2
    inner = query_key_value_matrix.shape[2]
    block = width // 128

    def vmem(*shape):
        return pltpu.VMEM(shape, jnp.float32)

    def short(*shape):
        return jax.ShapeDtypeStruct(shape, jnp.bfloat16)

    def full(*shape):
        return jax.ShapeDtypeStruct(shape, jnp.float32)

    def in_hbm(values):
        return pltpu.with_memory_space_constraint(values, pltpu.HBM)

    second_rows = second_factor_matrix.T
    first_rows = first_factor_matrix.T
    product_rows = product_result_matrix.transpose(1, 2, 0).reshape(-1, C_Z)
    (
        tile_piece,
        weight_piece,
        pair_field,
        sum_weights,
        gain_one,
        gain_two,
        first_rows,
        offset,
        chain_column,
        chain_gain,
        place,
        present,
    ) = call(
        functools.partial(prepare, extent, rows),
        (
            short(lines + 8, width),
            short(6 + product_rows.size // (inner * width), inner, width),
            short(slots, channels, cells),
            short(4 * heads, channels),
            full(1, width),
            full(1, width),
            short(features, width),
            full(channels, 128),
            full(extent, 128),
            full(heads, 128),
            jax.ShapeDtypeStruct((slots, 128), jnp.int32),
            full(slots, 128),
        ),
        jax.tree.map(
            in_hbm,
            (
            sequence_matrix,
            couple_matrix,
            query_key_value_matrix.transpose(0, 2, 1),
            focus_result_matrix,
            second_rows,
            amino_strand.reshape(1, extent),
            couple_scaling_factor.reshape(1, channels),
            focus_offset_matrix.T,
            sequence_scaling_factor.reshape(1, width),
            product_scaling_factor.reshape(1, width),
            first_rows,
            product_result_offset.reshape(1, channels),
            strand_focus_offset.reshape(1, heads),
            product_rows,
            block_target_entry,
            block_present_flag,
            ),
        ),
        [pl.BlockSpec(memory_space=pltpu.HBM)] * 16,
        [
            pltpu.VMEM(second_rows.shape, jnp.bfloat16),
            pltpu.VMEM((1, extent), jnp.int32),
            vmem(1, channels),
            vmem(heads, channels),
            pltpu.VMEM((features, width), jnp.bfloat16),
            vmem(1, channels),
            vmem(1, heads),
            pltpu.SMEM((1, slots), jnp.int32),
            pltpu.SMEM((1, slots), jnp.int32),
            vmem(block, features, 128),
            vmem(extent, 128),
            pltpu.SemaphoreType.DMA((14 + rows + product_rows.shape[0] // inner,)),
        ],
        1_000_000,
        3_000_000,
    )

    weight_pieces = over_groups(weight_piece, True)

    tile_pieces = over_tiles(tile_piece)

    sums_shape = (slots // 2, heads, cells + cells // (heads // 2) + 128)

    def sums_of(keep):
        return call(
            functools.partial(pair_sums, keep),
            jax.ShapeDtypeStruct(sums_shape, jnp.float32),
            (sum_weights, pair_field),
            [spec()] * 2,
            [],
            2 * slots // 2 * cells * channels * 4 * heads,
            couple_matrix.size,
        )

    given = sums_of(False)
    taken = flip(given, "ch", 1)
    kept = sums_of(True)
    merged, sent = call(
        functools.partial(merge_sums, channels),
        (full(*sums_shape[1:]), full(*sums_shape[1:])),
        (kept, taken),
        [spec()] * 2,
        [],
        given.size * 4,
        given.size * 12,
    )
    far_sums = flip(sent, "ch", 2)
    own_bias = call(
        functools.partial(pair_bias, extent),
        short(heads * half, 128),
        (merged, far_sums),
        [spec()] * 2,
        [vmem(heads * half, 128)],
        given.size * 4,
        given.size * 8,
    )
    bias_pieces = over_groups(own_bias, True)

    own_weights = call(
        product_tables,
        short(channels // 2, 128, 256),
        tuple(weight_pieces),
        [spec()] * 4,
        [
            vmem(groups, features, features // groups, C_Z),
            vmem(C_Z, 128),
            vmem(channels * features // 4, 128),
        ],
        1_000_000,
        2_000_000,
    )

    keys, values, query, gates, key_chain = call(
        functools.partial(project, extent, rows, tiles),
        (
            short(rows, slots * extent, width),
            short(rows, slots * extent, width),
            full(block, lines, 128),
            short(lines, width),
            full(slots, 8, 128),
        ),
        (place, *tile_pieces, *weight_pieces, gain_one),
        [spec()] * (tiles + 6),
        [pltpu.VMEM((tiles, lines + 8, width), jnp.bfloat16)],
        200_000_000,
        2_000_000,
    )
    row_piece, right_piece = call(
        functools.partial(attention, extent, rows),
        (short(lines, width), short(features, lines)),
        (
            keys,
            values,
            query,
            gates,
            key_chain,
            tile_piece,
            *weight_pieces,
            *bias_pieces,
            chain_column,
            chain_gain,
            gain_two,
            present,
        ),
        [spec()] * 18,
        [
            pltpu.VMEM((slots, heads * half, 128), jnp.bfloat16),
            vmem(2, heads * half, slots * extent),
            vmem(block, lines, 128),
        ],
        600_000_000,
        3_000_000,
    )

    right_pieces = [right_piece] + [flip(right_piece, "res", bits) for bits in range(2, tiles, 2)]
    stacked = jnp.stack(right_pieces)
    turned = flip(stacked, "res", 1)
    picked = call(
        pick,
        short(slots, features, lines),
        (place, stacked, turned),
        [spec()] * 3,
        [],
        1000,
        200_000,
    )
    right_tiles = over_groups(picked, False)
    row_pieces = over_groups(row_piece, False)

    table, sequence_result_matrix = call(
        functools.partial(left_tables, extent, rows),
        (
            short(half * channels, 2 * rows * 128),
            short(sequences, extent, width),
        ),
        (*row_pieces, first_rows, gain_two, own_weights),
        [spec()] * 7,
        [vmem(2 * rows, half * channels, 128), vmem(lines, 128)],
        300_000_000,
        3_000_000,
    )

    steps = 8
    pairwise_output = pl.pallas_call(
        functools.partial(pair_update, extent, rows, 1.0 / sequences),
        out_shape=jax.ShapeDtypeStruct(couple_matrix.shape, jnp.bfloat16),
        in_specs=[spec()] * 8,
        out_specs=pl.BlockSpec(memory_space=pl.ANY),
        scratch_shapes=[
            pltpu.VMEM((table.shape[1], slots * 128), jnp.bfloat16),
            pltpu.VMEM(couple_matrix.shape, jnp.bfloat16),
            pltpu.SemaphoreType.DMA((steps,)),
        ],
        name="pair_update",
        cost_estimate=pl.CostEstimate(
            flops=600_000_000, bytes_accessed=3_000_000, transcendentals=0
        ),
        compiler_params=pltpu.CompilerParams(vmem_limit_bytes=VMEM_LIMIT),
    )(present, table, pair_field, offset, *right_tiles)
    return (sequence_result_matrix, pairwise_output)


def solution(mesh):
    few = mesh.shape["res"] <= 8 and mesh.shape["ch"] == 4
    return jax.shard_map(
        on_device_small if few else on_device,
        mesh=mesh,
        in_specs=(
            P(None, "res", None),
            P("res", "ch", None),
            P("res", None),
            P("res", None),
            P("res"),
            P(),
            P(None, None, "ch"),
            P("ch", None),
            P(),
            P("ch"),
            P("ch", None),
            P(),
            P(),
            P(None, "ch"),
            P(None, None, "ch"),
            P("ch"),
        ),
        out_specs=(P(None, "res", None), P("res", "ch", None)),
        check_vma=False,
    )
```

```python
import functools
import math

import jax
import jax.numpy as jnp
from jax import lax
from jax.experimental import pallas as pl
from jax.experimental.pallas import tpu as pltpu
from jax.sharding import PartitionSpec as P


C_Z = 128
FOCUS_NUMBER = 8
FOCUS_BREADTH = 32
PRODUCT_FEATURE = 32


EPS = 1e-05
MASKED = -1e30


def final_dimension_standardize(values, gain_vector):
    values = values.astype(jnp.float32)
    average = jnp.mean(values, axis=-1, keepdims=True)
    variance = jnp.mean(jnp.square(values - average), axis=-1, keepdims=True)
    return (values - average) * lax.rsqrt(variance + EPS) * gain_vector


def on_device(
    sequence_matrix,
    couple_matrix,
    block_target_entry,
    block_present_flag,
    amino_strand,
    sequence_scaling_factor,
    query_key_value_matrix,
    focus_result_matrix,
    strand_focus_offset,
    couple_scaling_factor,
    focus_offset_matrix,
    product_scaling_factor,
    first_factor_matrix,
    second_factor_matrix,
    product_result_matrix,
    product_result_offset,
):
    groups = lax.axis_size("ch")
    group_index = lax.axis_index("ch")
    local_heads = FOCUS_NUMBER // groups
    slot_count = couple_matrix.shape[0]
    cell_count = couple_matrix.shape[2]
    block_extent = sequence_matrix.shape[1]
    sequence_number_overall = sequence_matrix.shape[0]
    pair_field = couple_matrix.astype(jnp.float32)
    part_one = jnp.sum(pair_field, axis=1)
    part_two = jnp.sum(pair_field * pair_field, axis=1)
    sum_one, sum_two = lax.psum((part_one, part_two), "ch")
    center = sum_one / C_Z
    spread = lax.rsqrt(sum_two / C_Z - center * center + EPS)
    normed = (
        (pair_field - center[:, None, :])
        * spread[:, None, :]
        * couple_scaling_factor[None, :, None]
    )
    partial_value = jnp.einsum(
        "kcp,ch->hkp", normed, focus_offset_matrix, precision=lax.Precision.HIGHEST
    )
    head_bias = lax.psum_scatter(partial_value, "ch", scatter_dimension=0, tiled=True)
    head_bias = head_bias.astype(jnp.bfloat16)
    bias_all, cols_all, valid_all, chain_all = (
        lax.all_gather(head_bias, "res", axis=1, tiled=True),
        lax.all_gather(block_target_entry, "res", axis=0, tiled=True),
        lax.all_gather(block_present_flag, "res", axis=0, tiled=True),
        lax.all_gather(amino_strand, "res", axis=0, tiled=True),
    )
    sequence_first_layout = lax.all_to_all(
        sequence_matrix, "res", split_axis=0, concat_axis=1, tiled=True
    )
    device_rows, amino_number_here, sequence_feature_breadth = sequence_first_layout.shape
    tile_count = amino_number_here // block_extent
    sequence_standardized = final_dimension_standardize(
        sequence_first_layout, sequence_scaling_factor
    ).astype(jnp.bfloat16)
    projected_rows = jnp.einsum(
        "hbx,sxt->shbt",
        sequence_standardized,
        query_key_value_matrix,
        preferred_element_type=jnp.float32,
    ).astype(jnp.bfloat16)
    projected_rows = projected_rows.reshape(
        4, device_rows, tile_count, block_extent, local_heads, FOCUS_BREADTH
    )
    queries = projected_rows[0]
    keyset = projected_rows[1]
    valueset = projected_rows[2]
    gateset = projected_rows[3]
    chain_tiles = chain_all.reshape(tile_count, block_extent)
    bias_tiles = bias_all.reshape(local_heads, tile_count, slot_count, block_extent, block_extent)
    head_scale = lax.dynamic_slice_in_dim(
        strand_focus_offset, group_index * local_heads, local_heads, 0
    )
    block_tiles = math.gcd(tile_count, max(1, 512 // block_extent))

    def attend(block_index):
        first_tile = block_index * block_tiles
        columns = lax.dynamic_slice_in_dim(cols_all, first_tile, block_tiles, 0)
        usable = lax.dynamic_slice_in_dim(valid_all, first_tile, block_tiles, 0) > 0
        query_block = lax.dynamic_slice_in_dim(queries, first_tile, block_tiles, 1)
        key_block = keyset[:, columns]
        value_block = valueset[:, columns]
        scores = jnp.einsum(
            "rgahd,rgkbhd->rghakb", query_block, key_block, preferred_element_type=jnp.float32
        ) * FOCUS_BREADTH ** (-0.5)
        pair_part = lax.dynamic_slice_in_dim(bias_tiles, first_tile, block_tiles, 1).astype(
            jnp.float32
        )
        pair_part = pair_part.transpose(1, 0, 3, 2, 4)
        query_chain = lax.dynamic_slice_in_dim(chain_tiles, first_tile, block_tiles, 0)
        same_chain = (query_chain[:, :, None, None] == chain_tiles[columns][:, None, :, :]).astype(
            jnp.float32
        )
        scores = (
            scores
            + pair_part[None]
            + head_scale[None, None, :, None, None, None] * same_chain[None, :, None]
        )
        scores = jnp.where(usable[None, :, None, None, :, None], scores, MASKED)
        row_max = jnp.max(scores, axis=(4, 5), keepdims=True)
        exponent = jnp.exp(scores - row_max)
        attn_weights = (exponent / jnp.sum(exponent, axis=(4, 5), keepdims=True)).astype(
            jnp.bfloat16
        )
        mixed = jnp.einsum(
            "rghakb,rgkbhd->rgahd", attn_weights, value_block, preferred_element_type=jnp.float32
        )
        gate_block = lax.dynamic_slice_in_dim(gateset, first_tile, block_tiles, 1).astype(
            jnp.float32
        )
        return (mixed * jax.nn.sigmoid(gate_block)).astype(jnp.bfloat16)

    blocks = lax.map(attend, jnp.arange(tile_count // block_tiles, dtype=jnp.int32))
    attended_rows = blocks.transpose(1, 0, 2, 3, 4, 5).reshape(
        device_rows * amino_number_here, local_heads * FOCUS_BREADTH
    )
    residual_input = sequence_first_layout.reshape(
        device_rows * amino_number_here, sequence_feature_breadth
    )
    partial_out = jnp.dot(attended_rows, focus_result_matrix, preferred_element_type=jnp.float32)
    head_total = lax.psum(partial_out, "ch")
    updated_state = (
        (residual_input.astype(jnp.float32) + head_total)
        .astype(jnp.bfloat16)
        .reshape(device_rows, amino_number_here, sequence_feature_breadth)
    )
    sequence_result_matrix = lax.all_to_all(
        updated_state, "res", split_axis=1, concat_axis=0, tiled=True
    )
    outer_normed = (
        final_dimension_standardize(sequence_result_matrix, product_scaling_factor)
        .astype(jnp.bfloat16)
        .reshape(sequence_number_overall * block_extent, sequence_feature_breadth)
    )
    left_projected = (
        jnp.dot(outer_normed, first_factor_matrix, preferred_element_type=jnp.float32)
        .astype(jnp.bfloat16)
        .reshape(sequence_number_overall, block_extent * PRODUCT_FEATURE)
    )
    own_columns = block_target_entry[0]
    right_projected = (
        jnp.dot(outer_normed, second_factor_matrix, preferred_element_type=jnp.float32)
        .astype(jnp.bfloat16)
        .reshape(sequence_number_overall, block_extent, -1)
    )
    narrow = right_projected.shape[2]
    weight_flat = product_result_matrix.reshape(C_Z, PRODUCT_FEATURE * narrow)
    empty_tiles = jnp.zeros(
        (slot_count, sequence_number_overall, block_extent, narrow), jnp.bfloat16
    )
    shard_piece = lax.all_gather(right_projected, "res", axis=1, tiled=True)
    piece_rows = shard_piece.shape[1]
    offset = own_columns * block_extent
    inside = (offset >= 0) & (offset < piece_rows)

    def take_one(offset_one, inside_one, held_tile):
        taken = lax.dynamic_slice_in_dim(
            shard_piece, jnp.clip(offset_one, 0, piece_rows - block_extent), block_extent, 1
        )
        return jnp.where(inside_one, taken, held_tile)

    chosen = jax.vmap(take_one, in_axes=(0, 0, 0))(offset, inside, empty_tiles)
    left_turned = left_projected.T

    def outer_one(right_tile_rows):
        product = (
            jnp.dot(
                left_turned,
                right_tile_rows.reshape(sequence_number_overall, block_extent * narrow),
                preferred_element_type=jnp.float32,
            )
            / sequence_number_overall
        )
        product = (
            product.reshape(block_extent, PRODUCT_FEATURE, block_extent, narrow)
            .transpose(1, 3, 0, 2)
            .astype(jnp.bfloat16)
            .reshape(PRODUCT_FEATURE * narrow, cell_count)
        )
        return jnp.dot(weight_flat, product, preferred_element_type=jnp.float32)

    partials = lax.map(outer_one, chosen)
    summed = lax.psum_scatter(partials, "ch", scatter_dimension=1, tiled=True)
    keep_mask = block_present_flag[0].astype(jnp.float32)
    pairwise_output = (
        pair_field + keep_mask[:, None, None] * (summed + product_result_offset[None, :, None])
    ).astype(jnp.bfloat16)
    return (sequence_result_matrix, pairwise_output)


ACROSS = (((1,), (0,)), ((), ()))
BOTH_LAST = (((1,), (1,)), ((), ()))
VMEM_LIMIT = 12 * 1024 * 1024


def flip(values, axis, bits):
    size = lax.axis_size(axis)
    return lax.ppermute(values, axis, [(i, i ^ bits) for i in range(size)])


def over_groups(values, relay):
    across = flip(values, "ch", 2)
    near = flip(values, "ch", 1)
    if relay:
        far = flip(across, "ch", 1)
    else:
        far = flip(values, "ch", 3)
    return [values, near, across, far]


def over_tiles(values):
    size = lax.axis_size("res")
    found = {0: values}
    for bits in range(size - 2, 0, -2):
        found[bits] = flip(values, "res", bits)
    for bits in range(0, size, 2):
        found[bits + 1] = flip(found[bits], "res", 1)
    return [found[bits] for bits in range(size)]


def dot(a, b, dims):
    return lax.dot_general(a, b, dims, preferred_element_type=jnp.float32)


def lane_block(shape, width):
    return lax.broadcasted_iota(jnp.int32, shape, len(shape) - 1) // width


def standardized(values, gain):
    average = jnp.mean(values, axis=-1, keepdims=True)
    centred = values - average
    variance = jnp.mean(centred * centred, axis=-1, keepdims=True)
    return centred * lax.rsqrt(variance + EPS) * gain


def put(ref, values):
    for b in range(ref.shape[0]):
        ref[b] = values[:, b * 128 : (b + 1) * 128]


def take(ref):
    return jnp.concatenate([ref[b] for b in range(ref.shape[0])], axis=1)


def put_every(ref, start, step, values, first=0):
    for b in range(values.shape[1] // 128):
        ref[first + b, pl.ds(start, values.shape[0], stride=step), :] = values[
            :, b * 128 : (b + 1) * 128
        ]


def take_every(ref, start, size, step):
    return jnp.concatenate(
        [ref[b, pl.ds(start, size, stride=step), :] for b in range(ref.shape[0])], axis=1
    )


def spec():
    return pl.BlockSpec(memory_space=pltpu.VMEM)


def call(body, out, inputs, specs, scratch, flops, moved):
    out_specs = jax.tree.map(lambda _: spec(), out)
    return pl.pallas_call(
        body,
        out_shape=out,
        in_specs=specs,
        out_specs=out_specs,
        scratch_shapes=scratch,
        cost_estimate=pl.CostEstimate(flops=flops, bytes_accessed=moved, transcendentals=0),
        compiler_params=pltpu.CompilerParams(vmem_limit_bytes=VMEM_LIMIT),
    )(*inputs)


def column(row, lanes):
    return jnp.broadcast_to(row, (lanes, row.shape[1])).T


def prepare(extent, rows, *refs):
    sources, outs, scratch = refs[:16], refs[16:28], refs[28:]
    sequence, pair, query_key_value, out_weight, second, strand = sources[:6]
    gain_pair, focus, gain_one, gain_two, first, offset, chain_gain = sources[6:13]
    product, target, present = sources[13:]
    tile_ref, weight_ref, pair_ref, sum_weight_ref, gain_one_ref, gain_two_ref = outs[:6]
    first_ref, offset_ref, chain_ref, chain_gain_ref, place_ref, open_ref = outs[6:]
    held_second, held_strand, held_gain, held_focus, held_first, held_offset = scratch[:6]
    held_chain_gain, held_target, held_present, wide, tall, sems = scratch[6:]
    lines = rows * extent
    group = lax.axis_index("ch")
    narrow = second.shape[0]
    moves = [
        (strand, held_strand),
        (second, held_second),
        (gain_pair, held_gain),
        (focus, held_focus),
        (first, held_first),
        (offset, held_offset),
        (chain_gain, held_chain_gain),
        (target, held_target),
        (present, held_present),
        (gain_one, gain_one_ref),
        (gain_two, gain_two_ref),
        (out_weight, weight_ref.at[4]),
        (query_key_value, weight_ref.at[0:4]),
        (pair, pair_ref),
    ]
    deep = weight_ref.shape[1]
    for i in range(product.shape[0] // deep):
        part = pl.ds((i % 2) * 128, 128)
        moves.append(
            (product.at[pl.ds(i * deep, deep)], weight_ref.at[6 + i // 2, :, part])
        )
    for s in range(rows):
        moves.append(
            (sequence.at[group * rows + s], tile_ref.at[s * extent : (s + 1) * extent])
        )
    copies = [
        pltpu.make_async_copy(source, target, sems.at[i])
        for i, (source, target) in enumerate(moves)
    ]
    for copy in copies:
        copy.start()
    for copy in copies[:9]:
        copy.wait()
    width = tile_ref.shape[1]
    tile = lax.axis_index("res")
    slots = target.shape[1]
    for k in range(slots):
        place_ref[k : k + 1, :] = jnp.full((1, 128), held_target[0, k] ^ tile)
        open_ref[k : k + 1, :] = jnp.full((1, 128), held_present[0, k]).astype(jnp.float32)
    chain = held_strand[...].astype(jnp.float32)
    twice = jnp.concatenate([chain] * (128 // extent), axis=1)
    line = jnp.broadcast_to(jnp.concatenate([twice] * (width // 128), axis=1), (8, width))
    tile_ref[lines:, :] = line.astype(jnp.bfloat16)
    tall[...] = column(chain, 128)
    half = extent // 2
    for p in range(2):
        chain_ref[p * half : (p + 1) * half, :] = tall[pl.ds(p, half, stride=2), :]
    spread = lax.broadcasted_iota(jnp.int32, (weight_ref.shape[1], width), 0)
    factor = jnp.concatenate(
        [held_second[...].astype(jnp.float32)] * (weight_ref.shape[1] // narrow), axis=0
    )
    weight_ref[5] = jnp.where(spread // narrow == group, factor, 0.0).astype(jnp.bfloat16)
    gains = held_focus[...] * held_gain[...]
    one = gains.astype(jnp.bfloat16).astype(jnp.float32)
    two = (gains - one).astype(jnp.bfloat16).astype(jnp.float32)
    sum_weight_ref[...] = jnp.concatenate(
        [one, two, gains - one - two, jnp.ones_like(gains)], axis=0
    ).astype(jnp.bfloat16)
    put(wide, held_first[...].astype(jnp.float32))
    features = first_ref.shape[0]
    first_ref[...] = jnp.concatenate(
        [take_every(wide, i, features // 4, 4) for i in range(4)], axis=0
    ).astype(jnp.bfloat16)
    offset_ref[...] = column(held_offset[...], 128)
    chain_gain_ref[...] = column(held_chain_gain[...], 128)
    for copy in copies[9:]:
        copy.wait()


def pair_sums(keep, weight_ref, pair_ref, out_ref):
    slots = pair_ref.shape[0] // 2
    channels, cells = pair_ref.shape[1:]
    odd = lax.rem(lax.axis_index("ch"), 2)
    half = odd if keep else 1 - odd
    weights = weight_ref[...]
    heads = FOCUS_NUMBER
    pieces = heads // 2
    stretch = cells // pieces
    total = jnp.sum(weights.astype(jnp.float32), axis=1, keepdims=True)
    gain = total[0:heads] + total[heads : 2 * heads] + total[2 * heads : 3 * heads]
    step = 512
    for k in range(slots):
        slot = half * slots + k
        for start in range(0, cells, step):
            part = pl.ds(start, step)
            block = pair_ref[slot, :, part]
            sums = dot(weights, block, ACROSS)
            mean = sums[3 * heads : 3 * heads + 1] * (1.0 / channels)
            head = sums[0:heads] + sums[heads : 2 * heads] + sums[2 * heads : 3 * heads]
            centred = block.astype(jnp.float32) - mean
            out_ref[k, :, part] = head - mean * gain
            piece = start // stretch
            line = pl.ds(cells + start % stretch, step)
            out_ref[k, piece : piece + 1, line] = mean
            out_ref[k, pieces + piece : pieces + piece + 1, line] = jnp.sum(
                centred * centred, axis=0, keepdims=True
            )
        out_ref[k, :, cells + stretch :] = jnp.broadcast_to(gain, (heads, 128))


def merge_sums(count, own_ref, other_ref, kept_ref, sent_ref):
    heads, width = kept_ref.shape
    pieces = heads // 2
    stretch = (width - 128) // (pieces + 1)
    cells = pieces * stretch
    high = lax.axis_index("ch") // 2
    step = 512
    for slot, out_ref in ((high, kept_ref), (1 - high, sent_ref)):
        gain_own = own_ref[slot, :, cells + stretch :]
        gain_other = other_ref[slot, :, cells + stretch :]
        half_gain = 0.5 * (gain_own - gain_other)[:, 0:1]
        out_ref[:, cells + stretch :] = gain_own + gain_other
        for start in range(cells, cells + stretch, step):
            part = pl.ds(start, step)
            own = own_ref[slot, :, part]
            other = other_ref[slot, :, part]
            apart = (own - other)[0:pieces]
            both = own + other
            out_ref[:, part] = jnp.concatenate(
                [0.5 * both[0:pieces], both[pieces:] + apart * apart * (0.5 * count)], axis=0
            )
        for start in range(0, cells, step):
            part = pl.ds(start, step)
            piece = start // stretch
            line = pl.ds(cells + start % stretch, step)
            apart = (
                own_ref[slot, piece : piece + 1, line] - other_ref[slot, piece : piece + 1, line]
            )
            out_ref[:, part] = own_ref[slot, :, part] + other_ref[slot, :, part] + apart * half_gain


def pair_bias(extent, own_ref, far_ref, out_ref, lines):
    heads, width = own_ref.shape
    half = extent // 2
    pieces = heads // 2
    stretch = (width - 128) // (pieces + 1)
    cells = pieces * stretch
    gain = own_ref[:, cells + stretch :] - far_ref[:, cells + stretch :]
    half_gain = 0.5 * gain[:, 0:1]
    step = 512
    for start in range(0, cells, step):
        part = pl.ds(start, step)
        piece = start // stretch
        line = pl.ds(cells + start % stretch, step)
        mean = slice(piece, piece + 1)
        square = slice(pieces + piece, pieces + piece + 1)
        apart = own_ref[mean, line] - far_ref[mean, line]
        spread = own_ref[square, line] + far_ref[square, line] + apart * apart * (C_Z / 4.0)
        inverse = lax.rsqrt(spread * (1.0 / C_Z) + EPS)
        head = (own_ref[:, part] + far_ref[:, part] + apart * half_gain) * inverse
        for inner in range(step // 128):
            lines[pl.ds(start // 128 + inner, heads, stride=half), :] = head[
                :, inner * 128 : (inner + 1) * 128
            ]
    out_ref[...] = lines[...].astype(jnp.bfloat16)


def project(extent, rows, tiles, place_ref, *refs):
    tile_refs, weight_refs = refs[:tiles], refs[tiles : tiles + 4]
    gain_ref, chain_ref, chain_gain_ref, open_ref = refs[tiles + 4 : tiles + 8]
    value_ref, gate_ref, score_ref, stack, key_rows, query = refs[tiles + 8 :]
    lines = rows * extent
    half = extent // 2
    heads = FOCUS_NUMBER
    local_heads = heads // 4
    slots = place_ref.shape[0]
    width = gate_ref.shape[1]
    group = lax.axis_index("ch")
    for m in range(tiles):
        stack[m] = tile_refs[m][...]
    gain = gain_ref[...]
    weights = [
        jnp.concatenate([ref[kind] for ref in weight_refs], axis=0) for kind in range(4)
    ]
    key_chain = []
    for k in range(slots):
        place = place_ref[k, 0]
        tile = stack[place, 0:lines, :].astype(jnp.float32)
        key_chain.append(stack[place, lines : lines + 8, 0:128].astype(jnp.float32)[0:1])
        normed = standardized(tile, gain).astype(jnp.bfloat16)
        if k == 0:
            asked = dot(normed, weights[0], BOTH_LAST).astype(jnp.bfloat16)
            put(query, asked.astype(jnp.float32))
            gate_ref[...] = dot(normed, weights[3], BOTH_LAST).astype(jnp.bfloat16)
        keys = dot(normed, weights[1], BOTH_LAST).astype(jnp.bfloat16)
        values = dot(normed, weights[2], BOTH_LAST).astype(jnp.bfloat16)
        for s in range(rows):
            part = slice(s * extent, (s + 1) * extent)
            key_rows[s, k * extent : (k + 1) * extent, :] = keys[part]
            value_ref[s, k * extent : (k + 1) * extent, :] = values[part]
    low = lax.broadcasted_iota(jnp.int32, (half, 128), 1) < extent
    head_lane = lane_block((half, width), FOCUS_BREADTH)
    is_open, chain = [], []
    for k in range(0, slots, 2):
        is_open.append(jnp.where(low, open_ref[k : k + 1, :], open_ref[k + 1 : k + 2, :]) > 0.0)
        chain.append(jnp.where(low[0:1], key_chain[k], key_chain[k + 1]))
    for p in range(2):
        same = [
            (chain_ref[p * half : (p + 1) * half, :] == one).astype(jnp.float32)
            for one in chain
        ]
        for s in range(rows):
            asked = take_every(query, s * extent + p, half, 2)
            asked = jnp.concatenate(
                [jnp.where(head_lane == h, asked, 0.0) for h in range(heads)], axis=0
            ).astype(jnp.bfloat16)
            scores = dot(asked, key_rows[s], BOTH_LAST) * FOCUS_BREADTH ** (-0.5)
            for h in range(heads):
                index = (group ^ (h // local_heads)) * local_heads + h % local_heads
                gain_row = chain_gain_ref[pl.ds(index, 1), :]
                rows_h = slice(h * half, (h + 1) * half)
                for q in range(slots // 2):
                    lanes = slice(q * 128, (q + 1) * 128)
                    score_ref[s, p, rows_h, lanes] = jnp.where(
                        is_open[q], scores[rows_h, lanes] + gain_row * same[q], MASKED
                    )


def attention(extent, rows, *refs):
    value_ref, gate_ref, score_ref, tile_ref = refs[:4]
    weight_refs, bias_refs = refs[4:8], refs[8:12]
    gain_ref = refs[12]
    row_ref, right_ref, pair, bias, attended = refs[13:]
    slots = pair.shape[0]
    heads = FOCUS_NUMBER
    local_heads = heads // 4
    width = row_ref.shape[1]
    half = extent // 2
    lines = rows * extent
    group = lax.axis_index("ch")
    for m in range(4):
        other = group ^ m
        pair[2 * lax.rem(other, 2) + other // 2] = bias_refs[m][...]

    low = lax.broadcasted_iota(jnp.int32, (half, 128), 1) < extent
    for k in range(0, slots, 2):
        lanes = slice((k // 2) * 128, (k // 2 + 1) * 128)
        for h in range(heads):
            rows_h = slice(h * half, (h + 1) * half)
            zero = pair[k, rows_h, :].astype(jnp.float32)
            one = pair[k + 1, rows_h, :].astype(jnp.float32)
            bias[0, rows_h, lanes] = jnp.where(low, zero, pltpu.roll(one, extent, 1))
            bias[1, rows_h, lanes] = jnp.where(low, pltpu.roll(zero, extent, 1), one)

    head_lane = lane_block((half, width), FOCUS_BREADTH)
    for s in range(rows):
        for p in range(2):
            parts = []
            for h in range(heads):
                index = (group ^ (h // local_heads)) * local_heads + h % local_heads
                start = pl.multiple_of(index * half, half)
                parts.append(
                    score_ref[s, p, h * half : (h + 1) * half, :]
                    + bias[p, pl.ds(start, half), :]
                )
            scores = jnp.concatenate(parts, axis=0)
            peak = jnp.max(scores, axis=1, keepdims=True)
            exponent = jnp.exp(scores - peak)
            share = 1.0 / jnp.sum(exponent, axis=1, keepdims=True)
            weight = (exponent * share).astype(jnp.bfloat16)
            mixed = dot(weight, value_ref[s], ACROSS)
            kept = jnp.zeros((half, width), jnp.float32)
            for h in range(heads):
                kept = kept + jnp.where(head_lane == h, mixed[h * half : (h + 1) * half], 0.0)
            put_every(attended, s * extent + p, 2, kept)
    gates = gate_ref[...].astype(jnp.float32)
    gated = (take(attended) * jax.nn.sigmoid(gates)).astype(jnp.bfloat16)
    out_weight = jnp.concatenate([ref[4] for ref in weight_refs], axis=0)
    change = dot(gated, out_weight, ACROSS)
    updated = (tile_ref[0:lines, :].astype(jnp.float32) + change).astype(jnp.bfloat16)
    row_ref[...] = updated
    opm = standardized(updated.astype(jnp.float32), gain_ref[...]).astype(jnp.bfloat16)
    factor = weight_refs[0][5].astype(jnp.float32)
    for ref in weight_refs[1:]:
        factor = factor + ref[5].astype(jnp.float32)
    factor = factor[0:PRODUCT_FEATURE].astype(jnp.bfloat16)
    right_ref[...] = dot(factor, opm, BOTH_LAST).astype(jnp.bfloat16)


def product_tables(*refs):
    piece_refs = refs[:4]
    table_ref, stack, turned, lined = refs[4:]
    features, narrow, channels = stack.shape[1:]
    share = channels // 4
    group = lax.axis_index("ch")
    deep = piece_refs[0].shape[1]
    for m in range(4):
        for i in range(features * narrow // deep):
            part = piece_refs[m][6 + i // 2, :, (i % 2) * 128 : (i % 2 + 1) * 128]
            few = deep // narrow
            stack[group ^ m, i * few : (i + 1) * few] = part.astype(
                jnp.float32
            ).reshape(few, narrow, channels)
    own = pl.multiple_of(group * share, share)
    lines = features // 4
    for block in range(lines):
        tall = jnp.concatenate(
            [
                stack[m, block * 4 + i]
                for i in range(4)
                for m in range(4)
            ],
            axis=0,
        )
        turned[...] = tall.T
        lined[pl.ds(block, share, stride=lines), :] = turned[pl.ds(own, share), :]
    lanes = lane_block((lines, 128), features)
    for z in range(share):
        rows = lined[z * lines : (z + 1) * lines, :]
        moved = [rows] + [pltpu.roll(rows, by * features, 1) for by in range(1, 4)]
        parts = [
            jnp.where(lanes == s, moved[(s - i) % 4], 0.0) for s in range(4) for i in range(4)
        ]
        table_ref[z // 2, :, (z % 2) * 128 : (z % 2 + 1) * 128] = jnp.concatenate(
            parts, axis=0
        ).astype(jnp.bfloat16)


def left_tables(extent, rows, *refs):
    piece_refs = refs[:4]
    factor_ref, gain_ref, weight_ref = refs[4:7]
    table_ref, result_ref = refs[7:9]
    spread, natural = refs[9:]
    half = extent // 2
    features = PRODUCT_FEATURE
    lines = rows * extent
    factor = jnp.concatenate([factor_ref[...]] * 4, axis=0)
    lanes = lane_block((lines, 128), features)
    left = jnp.zeros((lines, 128), jnp.float32)
    for m in range(4):
        piece = piece_refs[m][...]
        group = lax.axis_index("ch") ^ m
        for s in range(rows):
            result_ref[group * rows + s] = piece[s * extent : (s + 1) * extent]
        normed = standardized(piece.astype(jnp.float32), gain_ref[...]).astype(jnp.bfloat16)
        left = left + jnp.where(lanes == m, dot(normed, factor, BOTH_LAST), 0.0)
    natural[...] = left
    left = jnp.concatenate(
        [
            natural[pl.ds(s * extent + p, half, stride=2), :]
            for p in range(2)
            for s in range(rows)
        ],
        axis=0,
    ).astype(jnp.bfloat16)
    pairs = weight_ref.shape[0]
    for z in range(pairs):
        table = dot(left, weight_ref[z], ACROSS)
        for b in range(2 * rows):
            for q in range(2):
                spread[b, pl.ds(2 * z + q, half, stride=2 * pairs), :] = table[
                    b * half : (b + 1) * half, q * 128 : (q + 1) * 128
                ]
    for b in range(2 * rows):
        table_ref[:, b * 128 : (b + 1) * 128] = spread[b].astype(jnp.bfloat16)


def pick(place_ref, even_ref, odd_ref, out_ref):
    for k in range(out_ref.shape[0]):
        place = place_ref[k, 0]
        even = even_ref[place // 2]
        odd = odd_ref[place // 2]
        out_ref[k] = jnp.where(lax.rem(place, 2) == 0, even, odd)


def pair_update(extent, rows, scale, open_ref, table_ref, pair_ref, offset_ref, *refs):
    piece_refs = refs[:4]
    out_ref, right, held, sems = refs[4:]
    slots, channels, cells = pair_ref.shape
    low = lax.broadcasted_iota(jnp.int32, (4 * piece_refs[0].shape[1], 128), 1) < extent
    for k in range(slots):
        one = jnp.concatenate([ref[k] for ref in piece_refs], axis=0).astype(jnp.float32)
        turned = pltpu.roll(one, extent, 1)
        depth = one.shape[0]
        for p in range(2):
            for s in range(rows):
                value = one if s == p else turned
                value = jnp.where(low if p == 0 else jnp.logical_not(low), value, 0.0)
                start = (p * rows + s) * depth
                right[start : start + depth, k * 128 : (k + 1) * 128] = value.astype(
                    jnp.bfloat16
                )
    offset = offset_ref[...]
    keep = [open_ref[k : k + 1, :] for k in range(slots)]
    steps = sems.shape[0]
    stretch = cells // steps
    deep = stretch // 128
    copies = []
    for i in range(steps):
        total = dot(
            table_ref[i * deep * channels : (i + 1) * deep * channels, :], right[...], ACROSS
        )
        for k in range(slots):
            for line in range(deep):
                update = total[line * channels : (line + 1) * channels, k * 128 : (k + 1) * 128]
                update = update * scale + offset
                cell = slice((i * deep + line) * 128, (i * deep + line + 1) * 128)
                held[k, :, cell] = (
                    pair_ref[k, :, cell].astype(jnp.float32) + keep[k] * update
                ).astype(jnp.bfloat16)
        part = pl.ds(i * stretch, stretch)
        copies.append(
            pltpu.make_async_copy(held.at[:, :, part], out_ref.at[:, :, part], sems.at[i])
        )
        copies[-1].start()
    for copy in copies:
        copy.wait()


def on_device_small(*arguments):
    return small(*arguments)


def small(
    sequence_matrix,
    couple_matrix,
    block_target_entry,
    block_present_flag,
    amino_strand,
    sequence_scaling_factor,
    query_key_value_matrix,
    focus_result_matrix,
    strand_focus_offset,
    couple_scaling_factor,
    focus_offset_matrix,
    product_scaling_factor,
    first_factor_matrix,
    second_factor_matrix,
    product_result_matrix,
    product_result_offset,
):
    groups = lax.axis_size("ch")
    tiles = lax.axis_size("res")
    sequences, extent, width = sequence_matrix.shape
    slots, channels, cells = couple_matrix.shape
    rows = sequences // groups
    lines = rows * extent
    heads = FOCUS_NUMBER
    features = PRODUCT_FEATURE
    half = extent // 2
    inner = query_key_value_matrix.shape[2]
    block = width // 128

    def vmem(*shape):
        return pltpu.VMEM(shape, jnp.float32)

    def short(*shape):
        return jax.ShapeDtypeStruct(shape, jnp.bfloat16)

    def full(*shape):
        return jax.ShapeDtypeStruct(shape, jnp.float32)

    def in_hbm(values):
        return pltpu.with_memory_space_constraint(values, pltpu.HBM)

    second_rows = second_factor_matrix.T
    first_rows = first_factor_matrix.T
    product_rows = product_result_matrix.transpose(1, 2, 0).reshape(-1, C_Z)
    (
        tile_piece,
        weight_piece,
        pair_field,
        sum_weights,
        gain_one,
        gain_two,
        first_rows,
        offset,
        chain_column,
        chain_gain,
        place,
        present,
    ) = call(
        functools.partial(prepare, extent, rows),
        (
            short(lines + 8, width),
            short(6 + product_rows.size // (inner * width), inner, width),
            short(slots, channels, cells),
            short(4 * heads, channels),
            full(1, width),
            full(1, width),
            short(features, width),
            full(channels, 128),
            full(extent, 128),
            full(heads, 128),
            jax.ShapeDtypeStruct((slots, 128), jnp.int32),
            full(slots, 128),
        ),
        jax.tree.map(
            in_hbm,
            (
            sequence_matrix,
            couple_matrix,
            query_key_value_matrix.transpose(0, 2, 1),
            focus_result_matrix,
            second_rows,
            amino_strand.reshape(1, extent),
            couple_scaling_factor.reshape(1, channels),
            focus_offset_matrix.T,
            sequence_scaling_factor.reshape(1, width),
            product_scaling_factor.reshape(1, width),
            first_rows,
            product_result_offset.reshape(1, channels),
            strand_focus_offset.reshape(1, heads),
            product_rows,
            block_target_entry,
            block_present_flag,
            ),
        ),
        [pl.BlockSpec(memory_space=pltpu.HBM)] * 16,
        [
            pltpu.VMEM(second_rows.shape, jnp.bfloat16),
            pltpu.VMEM((1, extent), jnp.int32),
            vmem(1, channels),
            vmem(heads, channels),
            pltpu.VMEM((features, width), jnp.bfloat16),
            vmem(1, channels),
            vmem(1, heads),
            pltpu.SMEM((1, slots), jnp.int32),
            pltpu.SMEM((1, slots), jnp.int32),
            vmem(block, features, 128),
            vmem(extent, 128),
            pltpu.SemaphoreType.DMA((14 + rows + product_rows.shape[0] // inner,)),
        ],
        1_000_000,
        3_000_000,
    )

    weight_pieces = over_groups(weight_piece, True)

    tile_pieces = over_tiles(tile_piece)

    sums_shape = (slots // 2, heads, cells + cells // (heads // 2) + 128)

    def sums_of(keep):
        return call(
            functools.partial(pair_sums, keep),
            jax.ShapeDtypeStruct(sums_shape, jnp.float32),
            (sum_weights, pair_field),
            [spec()] * 2,
            [],
            2 * slots // 2 * cells * channels * 4 * heads,
            couple_matrix.size,
        )

    given = sums_of(False)
    taken = flip(given, "ch", 1)
    kept = sums_of(True)
    merged, sent = call(
        functools.partial(merge_sums, channels),
        (full(*sums_shape[1:]), full(*sums_shape[1:])),
        (kept, taken),
        [spec()] * 2,
        [],
        given.size * 4,
        given.size * 12,
    )
    far_sums = flip(sent, "ch", 2)
    own_bias = call(
        functools.partial(pair_bias, extent),
        short(heads * half, 128),
        (merged, far_sums),
        [spec()] * 2,
        [vmem(heads * half, 128)],
        given.size * 4,
        given.size * 8,
    )
    bias_pieces = over_groups(own_bias, True)

    own_weights = call(
        product_tables,
        short(channels // 2, 128, 256),
        tuple(weight_pieces),
        [spec()] * 4,
        [
            vmem(groups, features, features // groups, C_Z),
            vmem(C_Z, 128),
            vmem(channels * features // 4, 128),
        ],
        1_000_000,
        2_000_000,
    )

    values, gates, scores = call(
        functools.partial(project, extent, rows, tiles),
        (
            short(rows, slots * extent, width),
            short(lines, width),
            full(rows, 2, heads * half, slots * extent),
        ),
        (
            place,
            *tile_pieces,
            *weight_pieces,
            gain_one,
            chain_column,
            chain_gain,
            present,
        ),
        [spec()] * (tiles + 9),
        [
            pltpu.VMEM((tiles, lines + 8, width), jnp.bfloat16),
            pltpu.VMEM((rows, slots * extent, width), jnp.bfloat16),
            vmem(block, lines, 128),
        ],
        200_000_000,
        2_000_000,
    )
    row_piece, right_piece = call(
        functools.partial(attention, extent, rows),
        (short(lines, width), short(features, lines)),
        (
            values,
            gates,
            scores,
            tile_piece,
            *weight_pieces,
            *bias_pieces,
            gain_two,
        ),
        [spec()] * 13,
        [
            pltpu.VMEM((slots, heads * half, 128), jnp.bfloat16),
            vmem(2, heads * half, slots * extent),
            vmem(block, lines, 128),
        ],
        600_000_000,
        3_000_000,
    )

    right_pieces = [right_piece] + [flip(right_piece, "res", bits) for bits in range(2, tiles, 2)]
    stacked = jnp.stack(right_pieces)
    turned = flip(stacked, "res", 1)
    picked = call(
        pick,
        short(slots, features, lines),
        (place, stacked, turned),
        [spec()] * 3,
        [],
        1000,
        200_000,
    )
    right_tiles = over_groups(picked, False)
    row_pieces = over_groups(row_piece, False)

    table, sequence_result_matrix = call(
        functools.partial(left_tables, extent, rows),
        (
            short(half * channels, 2 * rows * 128),
            short(sequences, extent, width),
        ),
        (*row_pieces, first_rows, gain_two, own_weights),
        [spec()] * 7,
        [vmem(2 * rows, half * channels, 128), vmem(lines, 128)],
        300_000_000,
        3_000_000,
    )

    steps = 8
    pairwise_output = pl.pallas_call(
        functools.partial(pair_update, extent, rows, 1.0 / sequences),
        out_shape=jax.ShapeDtypeStruct(couple_matrix.shape, jnp.bfloat16),
        in_specs=[spec()] * 8,
        out_specs=pl.BlockSpec(memory_space=pl.ANY),
        scratch_shapes=[
            pltpu.VMEM((table.shape[1], slots * 128), jnp.bfloat16),
            pltpu.VMEM(couple_matrix.shape, jnp.bfloat16),
            pltpu.SemaphoreType.DMA((steps,)),
        ],
        name="pair_update",
        cost_estimate=pl.CostEstimate(
            flops=600_000_000, bytes_accessed=3_000_000, transcendentals=0
        ),
        compiler_params=pltpu.CompilerParams(vmem_limit_bytes=VMEM_LIMIT),
    )(present, table, pair_field, offset, *right_tiles)
    return (sequence_result_matrix, pairwise_output)


def solution(mesh):
    few = mesh.shape["res"] <= 8 and mesh.shape["ch"] == 4
    return jax.shard_map(
        on_device_small if few else on_device,
        mesh=mesh,
        in_specs=(
            P(None, "res", None),
            P("res", "ch", None),
            P("res", None),
            P("res", None),
            P("res"),
            P(),
            P(None, None, "ch"),
            P("ch", None),
            P(),
            P("ch"),
            P("ch", None),
            P(),
            P(),
            P(None, "ch"),
            P(None, None, "ch"),
            P("ch"),
        ),
        out_specs=(P(None, "res", None), P("res", "ch", None)),
        check_vma=False,
    )
```

```python
import functools
import math

import jax
import jax.numpy as jnp
from jax import lax
from jax.experimental import pallas as pl
from jax.experimental.pallas import tpu as pltpu
from jax.sharding import PartitionSpec as P


C_Z = 128
FOCUS_NUMBER = 8
FOCUS_BREADTH = 32
PRODUCT_FEATURE = 32


EPS = 1e-05
MASKED = -1e30


def final_dimension_standardize(values, gain_vector):
    values = values.astype(jnp.float32)
    average = jnp.mean(values, axis=-1, keepdims=True)
    variance = jnp.mean(jnp.square(values - average), axis=-1, keepdims=True)
    return (values - average) * lax.rsqrt(variance + EPS) * gain_vector


def on_device(
    sequence_matrix,
    couple_matrix,
    block_target_entry,
    block_present_flag,
    amino_strand,
    sequence_scaling_factor,
    query_key_value_matrix,
    focus_result_matrix,
    strand_focus_offset,
    couple_scaling_factor,
    focus_offset_matrix,
    product_scaling_factor,
    first_factor_matrix,
    second_factor_matrix,
    product_result_matrix,
    product_result_offset,
):
    groups = lax.axis_size("ch")
    group_index = lax.axis_index("ch")
    local_heads = FOCUS_NUMBER // groups
    slot_count = couple_matrix.shape[0]
    cell_count = couple_matrix.shape[2]
    block_extent = sequence_matrix.shape[1]
    sequence_number_overall = sequence_matrix.shape[0]
    pair_field = couple_matrix.astype(jnp.float32)
    part_one = jnp.sum(pair_field, axis=1)
    part_two = jnp.sum(pair_field * pair_field, axis=1)
    sum_one, sum_two = lax.psum((part_one, part_two), "ch")
    center = sum_one / C_Z
    spread = lax.rsqrt(sum_two / C_Z - center * center + EPS)
    normed = (
        (pair_field - center[:, None, :])
        * spread[:, None, :]
        * couple_scaling_factor[None, :, None]
    )
    partial_value = jnp.einsum(
        "kcp,ch->hkp", normed, focus_offset_matrix, precision=lax.Precision.HIGHEST
    )
    head_bias = lax.psum_scatter(partial_value, "ch", scatter_dimension=0, tiled=True)
    head_bias = head_bias.astype(jnp.bfloat16)
    bias_all, cols_all, valid_all, chain_all = (
        lax.all_gather(head_bias, "res", axis=1, tiled=True),
        lax.all_gather(block_target_entry, "res", axis=0, tiled=True),
        lax.all_gather(block_present_flag, "res", axis=0, tiled=True),
        lax.all_gather(amino_strand, "res", axis=0, tiled=True),
    )
    sequence_first_layout = lax.all_to_all(
        sequence_matrix, "res", split_axis=0, concat_axis=1, tiled=True
    )
    device_rows, amino_number_here, sequence_feature_breadth = sequence_first_layout.shape
    tile_count = amino_number_here // block_extent
    sequence_standardized = final_dimension_standardize(
        sequence_first_layout, sequence_scaling_factor
    ).astype(jnp.bfloat16)
    projected_rows = jnp.einsum(
        "hbx,sxt->shbt",
        sequence_standardized,
        query_key_value_matrix,
        preferred_element_type=jnp.float32,
    ).astype(jnp.bfloat16)
    projected_rows = projected_rows.reshape(
        4, device_rows, tile_count, block_extent, local_heads, FOCUS_BREADTH
    )
    queries = projected_rows[0]
    keyset = projected_rows[1]
    valueset = projected_rows[2]
    gateset = projected_rows[3]
    chain_tiles = chain_all.reshape(tile_count, block_extent)
    bias_tiles = bias_all.reshape(local_heads, tile_count, slot_count, block_extent, block_extent)
    head_scale = lax.dynamic_slice_in_dim(
        strand_focus_offset, group_index * local_heads, local_heads, 0
    )
    block_tiles = math.gcd(tile_count, max(1, 512 // block_extent))

    def attend(block_index):
        first_tile = block_index * block_tiles
        columns = lax.dynamic_slice_in_dim(cols_all, first_tile, block_tiles, 0)
        usable = lax.dynamic_slice_in_dim(valid_all, first_tile, block_tiles, 0) > 0
        query_block = lax.dynamic_slice_in_dim(queries, first_tile, block_tiles, 1)
        key_block = keyset[:, columns]
        value_block = valueset[:, columns]
        scores = jnp.einsum(
            "rgahd,rgkbhd->rghakb", query_block, key_block, preferred_element_type=jnp.float32
        ) * FOCUS_BREADTH ** (-0.5)
        pair_part = lax.dynamic_slice_in_dim(bias_tiles, first_tile, block_tiles, 1).astype(
            jnp.float32
        )
        pair_part = pair_part.transpose(1, 0, 3, 2, 4)
        query_chain = lax.dynamic_slice_in_dim(chain_tiles, first_tile, block_tiles, 0)
        same_chain = (query_chain[:, :, None, None] == chain_tiles[columns][:, None, :, :]).astype(
            jnp.float32
        )
        scores = (
            scores
            + pair_part[None]
            + head_scale[None, None, :, None, None, None] * same_chain[None, :, None]
        )
        scores = jnp.where(usable[None, :, None, None, :, None], scores, MASKED)
        row_max = jnp.max(scores, axis=(4, 5), keepdims=True)
        exponent = jnp.exp(scores - row_max)
        attn_weights = (exponent / jnp.sum(exponent, axis=(4, 5), keepdims=True)).astype(
            jnp.bfloat16
        )
        mixed = jnp.einsum(
            "rghakb,rgkbhd->rgahd", attn_weights, value_block, preferred_element_type=jnp.float32
        )
        gate_block = lax.dynamic_slice_in_dim(gateset, first_tile, block_tiles, 1).astype(
            jnp.float32
        )
        return (mixed * jax.nn.sigmoid(gate_block)).astype(jnp.bfloat16)

    blocks = lax.map(attend, jnp.arange(tile_count // block_tiles, dtype=jnp.int32))
    attended_rows = blocks.transpose(1, 0, 2, 3, 4, 5).reshape(
        device_rows * amino_number_here, local_heads * FOCUS_BREADTH
    )
    residual_input = sequence_first_layout.reshape(
        device_rows * amino_number_here, sequence_feature_breadth
    )
    partial_out = jnp.dot(attended_rows, focus_result_matrix, preferred_element_type=jnp.float32)
    head_total = lax.psum(partial_out, "ch")
    updated_state = (
        (residual_input.astype(jnp.float32) + head_total)
        .astype(jnp.bfloat16)
        .reshape(device_rows, amino_number_here, sequence_feature_breadth)
    )
    sequence_result_matrix = lax.all_to_all(
        updated_state, "res", split_axis=1, concat_axis=0, tiled=True
    )
    outer_normed = (
        final_dimension_standardize(sequence_result_matrix, product_scaling_factor)
        .astype(jnp.bfloat16)
        .reshape(sequence_number_overall * block_extent, sequence_feature_breadth)
    )
    left_projected = (
        jnp.dot(outer_normed, first_factor_matrix, preferred_element_type=jnp.float32)
        .astype(jnp.bfloat16)
        .reshape(sequence_number_overall, block_extent * PRODUCT_FEATURE)
    )
    own_columns = block_target_entry[0]
    right_projected = (
        jnp.dot(outer_normed, second_factor_matrix, preferred_element_type=jnp.float32)
        .astype(jnp.bfloat16)
        .reshape(sequence_number_overall, block_extent, -1)
    )
    narrow = right_projected.shape[2]
    weight_flat = product_result_matrix.reshape(C_Z, PRODUCT_FEATURE * narrow)
    empty_tiles = jnp.zeros(
        (slot_count, sequence_number_overall, block_extent, narrow), jnp.bfloat16
    )
    shard_piece = lax.all_gather(right_projected, "res", axis=1, tiled=True)
    piece_rows = shard_piece.shape[1]
    offset = own_columns * block_extent
    inside = (offset >= 0) & (offset < piece_rows)

    def take_one(offset_one, inside_one, held_tile):
        taken = lax.dynamic_slice_in_dim(
            shard_piece, jnp.clip(offset_one, 0, piece_rows - block_extent), block_extent, 1
        )
        return jnp.where(inside_one, taken, held_tile)

    chosen = jax.vmap(take_one, in_axes=(0, 0, 0))(offset, inside, empty_tiles)
    left_turned = left_projected.T

    def outer_one(right_tile_rows):
        product = (
            jnp.dot(
                left_turned,
                right_tile_rows.reshape(sequence_number_overall, block_extent * narrow),
                preferred_element_type=jnp.float32,
            )
            / sequence_number_overall
        )
        product = (
            product.reshape(block_extent, PRODUCT_FEATURE, block_extent, narrow)
            .transpose(1, 3, 0, 2)
            .astype(jnp.bfloat16)
            .reshape(PRODUCT_FEATURE * narrow, cell_count)
        )
        return jnp.dot(weight_flat, product, preferred_element_type=jnp.float32)

    partials = lax.map(outer_one, chosen)
    summed = lax.psum_scatter(partials, "ch", scatter_dimension=1, tiled=True)
    keep_mask = block_present_flag[0].astype(jnp.float32)
    pairwise_output = (
        pair_field + keep_mask[:, None, None] * (summed + product_result_offset[None, :, None])
    ).astype(jnp.bfloat16)
    return (sequence_result_matrix, pairwise_output)


ACROSS = (((1,), (0,)), ((), ()))
BOTH_LAST = (((1,), (1,)), ((), ()))
VMEM_LIMIT = 12 * 1024 * 1024


def flip(values, axis, bits):
    size = lax.axis_size(axis)
    return lax.ppermute(values, axis, [(i, i ^ bits) for i in range(size)])


def over_groups(values, relay):
    across = flip(values, "ch", 2)
    near = flip(values, "ch", 1)
    if relay:
        far = flip(across, "ch", 1)
    else:
        far = flip(values, "ch", 3)
    return [values, near, across, far]


def over_tiles(values):
    size = lax.axis_size("res")
    found = {0: values}
    for bits in range(size - 2, 0, -2):
        found[bits] = flip(values, "res", bits)
    for bits in range(0, size, 2):
        found[bits + 1] = flip(found[bits], "res", 1)
    return [found[bits] for bits in range(size)]


def dot(a, b, dims):
    return lax.dot_general(a, b, dims, preferred_element_type=jnp.float32)


def lane_block(shape, width):
    return lax.broadcasted_iota(jnp.int32, shape, len(shape) - 1) // width


def standardized(values, gain):
    average = jnp.mean(values, axis=-1, keepdims=True)
    centred = values - average
    variance = jnp.mean(centred * centred, axis=-1, keepdims=True)
    return centred * lax.rsqrt(variance + EPS) * gain


def put(ref, values):
    for b in range(ref.shape[0]):
        ref[b] = values[:, b * 128 : (b + 1) * 128]


def take(ref):
    return jnp.concatenate([ref[b] for b in range(ref.shape[0])], axis=1)


def put_every(ref, start, step, values, first=0):
    for b in range(values.shape[1] // 128):
        ref[first + b, pl.ds(start, values.shape[0], stride=step), :] = values[
            :, b * 128 : (b + 1) * 128
        ]


def take_every(ref, start, size, step):
    return jnp.concatenate(
        [ref[b, pl.ds(start, size, stride=step), :] for b in range(ref.shape[0])], axis=1
    )


def spec():
    return pl.BlockSpec(memory_space=pltpu.VMEM)


def call(body, out, inputs, specs, scratch, flops, moved):
    out_specs = jax.tree.map(lambda _: spec(), out)
    return pl.pallas_call(
        body,
        out_shape=out,
        in_specs=specs,
        out_specs=out_specs,
        scratch_shapes=scratch,
        cost_estimate=pl.CostEstimate(flops=flops, bytes_accessed=moved, transcendentals=0),
        compiler_params=pltpu.CompilerParams(vmem_limit_bytes=VMEM_LIMIT),
    )(*inputs)


def column(row, lanes):
    return jnp.broadcast_to(row, (lanes, row.shape[1])).T


def prepare(extent, rows, *refs):
    sources, outs, scratch = refs[:16], refs[16:28], refs[28:]
    sequence, pair, query_key_value, out_weight, second, strand = sources[:6]
    gain_pair, focus, gain_one, gain_two, first, offset, chain_gain = sources[6:13]
    product, target, present = sources[13:]
    tile_ref, weight_ref, pair_ref, sum_weight_ref, gain_one_ref, gain_two_ref = outs[:6]
    first_ref, offset_ref, chain_ref, chain_gain_ref, place_ref, open_ref = outs[6:]
    held_second, held_strand, held_gain, held_focus, held_first, held_offset = scratch[:6]
    held_chain_gain, held_target, held_present, wide, tall, sems = scratch[6:]
    lines = rows * extent
    group = lax.axis_index("ch")
    narrow = second.shape[0]
    moves = [
        (strand, held_strand),
        (second, held_second),
        (gain_pair, held_gain),
        (focus, held_focus),
        (first, held_first),
        (offset, held_offset),
        (chain_gain, held_chain_gain),
        (target, held_target),
        (present, held_present),
        (gain_one, gain_one_ref),
        (gain_two, gain_two_ref),
        (out_weight, weight_ref.at[4]),
        (query_key_value, weight_ref.at[0:4]),
        (pair, pair_ref),
    ]
    deep = weight_ref.shape[1]
    for i in range(product.shape[0] // deep):
        part = pl.ds((i % 2) * 128, 128)
        moves.append(
            (product.at[pl.ds(i * deep, deep)], weight_ref.at[6 + i // 2, :, part])
        )
    for s in range(rows):
        moves.append(
            (sequence.at[group * rows + s], tile_ref.at[s * extent : (s + 1) * extent])
        )
    copies = [
        pltpu.make_async_copy(source, target, sems.at[i])
        for i, (source, target) in enumerate(moves)
    ]
    for copy in copies:
        copy.start()
    for copy in copies[:9]:
        copy.wait()
    width = tile_ref.shape[1]
    tile = lax.axis_index("res")
    slots = target.shape[1]
    for k in range(slots):
        place_ref[k : k + 1, :] = jnp.full((1, 128), held_target[0, k] ^ tile)
        open_ref[k : k + 1, :] = jnp.full((1, 128), held_present[0, k]).astype(jnp.float32)
    chain = held_strand[...].astype(jnp.float32)
    twice = jnp.concatenate([chain] * (128 // extent), axis=1)
    line = jnp.broadcast_to(jnp.concatenate([twice] * (width // 128), axis=1), (8, width))
    tile_ref[lines:, :] = line.astype(jnp.bfloat16)
    tall[...] = column(chain, 128)
    half = extent // 2
    for p in range(2):
        chain_ref[p * half : (p + 1) * half, :] = tall[pl.ds(p, half, stride=2), :]
    spread = lax.broadcasted_iota(jnp.int32, (weight_ref.shape[1], width), 0)
    factor = jnp.concatenate(
        [held_second[...].astype(jnp.float32)] * (weight_ref.shape[1] // narrow), axis=0
    )
    weight_ref[5] = jnp.where(spread // narrow == group, factor, 0.0).astype(jnp.bfloat16)
    gains = held_focus[...] * held_gain[...]
    one = gains.astype(jnp.bfloat16).astype(jnp.float32)
    two = (gains - one).astype(jnp.bfloat16).astype(jnp.float32)
    sum_weight_ref[...] = jnp.concatenate(
        [one, two, gains - one - two, jnp.ones_like(gains)], axis=0
    ).astype(jnp.bfloat16)
    put(wide, held_first[...].astype(jnp.float32))
    features = first_ref.shape[0]
    first_ref[...] = jnp.concatenate(
        [take_every(wide, i, features // 4, 4) for i in range(4)], axis=0
    ).astype(jnp.bfloat16)
    offset_ref[...] = column(held_offset[...], 128)
    chain_gain_ref[...] = column(held_chain_gain[...], 128)
    for copy in copies[9:]:
        copy.wait()


def pair_sums(keep, weight_ref, pair_ref, out_ref):
    slots = pair_ref.shape[0] // 2
    channels, cells = pair_ref.shape[1:]
    odd = lax.rem(lax.axis_index("ch"), 2)
    half = odd if keep else 1 - odd
    weights = weight_ref[...]
    heads = FOCUS_NUMBER
    pieces = heads // 2
    stretch = cells // pieces
    total = jnp.sum(weights.astype(jnp.float32), axis=1, keepdims=True)
    gain = total[0:heads] + total[heads : 2 * heads] + total[2 * heads : 3 * heads]
    step = 512
    for k in range(slots):
        slot = half * slots + k
        for start in range(0, cells, step):
            part = pl.ds(start, step)
            block = pair_ref[slot, :, part]
            sums = dot(weights, block, ACROSS)
            mean = sums[3 * heads : 3 * heads + 1] * (1.0 / channels)
            head = sums[0:heads] + sums[heads : 2 * heads] + sums[2 * heads : 3 * heads]
            centred = block.astype(jnp.float32) - mean
            out_ref[k, :, part] = head - mean * gain
            piece = start // stretch
            line = pl.ds(cells + start % stretch, step)
            out_ref[k, piece : piece + 1, line] = mean
            out_ref[k, pieces + piece : pieces + piece + 1, line] = jnp.sum(
                centred * centred, axis=0, keepdims=True
            )
        out_ref[k, :, cells + stretch :] = jnp.broadcast_to(gain, (heads, 128))


def merge_sums(count, own_ref, other_ref, kept_ref, sent_ref):
    heads, width = kept_ref.shape
    pieces = heads // 2
    stretch = (width - 128) // (pieces + 1)
    cells = pieces * stretch
    high = lax.axis_index("ch") // 2
    step = 512
    for slot, out_ref in ((high, kept_ref), (1 - high, sent_ref)):
        gain_own = own_ref[slot, :, cells + stretch :]
        gain_other = other_ref[slot, :, cells + stretch :]
        half_gain = 0.5 * (gain_own - gain_other)[:, 0:1]
        out_ref[:, cells + stretch :] = gain_own + gain_other
        for start in range(cells, cells + stretch, step):
            part = pl.ds(start, step)
            own = own_ref[slot, :, part]
            other = other_ref[slot, :, part]
            apart = (own - other)[0:pieces]
            both = own + other
            out_ref[:, part] = jnp.concatenate(
                [0.5 * both[0:pieces], both[pieces:] + apart * apart * (0.5 * count)], axis=0
            )
        for start in range(0, cells, step):
            part = pl.ds(start, step)
            piece = start // stretch
            line = pl.ds(cells + start % stretch, step)
            apart = (
                own_ref[slot, piece : piece + 1, line] - other_ref[slot, piece : piece + 1, line]
            )
            out_ref[:, part] = own_ref[slot, :, part] + other_ref[slot, :, part] + apart * half_gain


def pair_bias(extent, own_ref, far_ref, out_ref, lines):
    heads, width = own_ref.shape
    half = extent // 2
    pieces = heads // 2
    stretch = (width - 128) // (pieces + 1)
    cells = pieces * stretch
    gain = own_ref[:, cells + stretch :] - far_ref[:, cells + stretch :]
    half_gain = 0.5 * gain[:, 0:1]
    step = 512
    for start in range(0, cells, step):
        part = pl.ds(start, step)
        piece = start // stretch
        line = pl.ds(cells + start % stretch, step)
        mean = slice(piece, piece + 1)
        square = slice(pieces + piece, pieces + piece + 1)
        apart = own_ref[mean, line] - far_ref[mean, line]
        spread = own_ref[square, line] + far_ref[square, line] + apart * apart * (C_Z / 4.0)
        inverse = lax.rsqrt(spread * (1.0 / C_Z) + EPS)
        head = (own_ref[:, part] + far_ref[:, part] + apart * half_gain) * inverse
        for inner in range(step // 128):
            lines[pl.ds(start // 128 + inner, heads, stride=half), :] = head[
                :, inner * 128 : (inner + 1) * 128
            ]
    out_ref[...] = lines[...].astype(jnp.bfloat16)


def project(extent, rows, tiles, place_ref, *refs):
    tile_refs, weight_refs = refs[:tiles], refs[tiles : tiles + 4]
    gain_ref, chain_ref, chain_gain_ref, open_ref = refs[tiles + 4 : tiles + 8]
    value_ref, gate_ref, score_ref, stack, key_rows, query = refs[tiles + 8 :]
    lines = rows * extent
    half = extent // 2
    heads = FOCUS_NUMBER
    local_heads = heads // 4
    slots = place_ref.shape[0]
    width = gate_ref.shape[1]
    group = lax.axis_index("ch")
    for m in range(tiles):
        stack[m] = tile_refs[m][...]
    gain = gain_ref[...]
    weights = [
        jnp.concatenate([ref[kind] for ref in weight_refs], axis=0) for kind in range(4)
    ]
    key_chain = []
    for k in range(slots):
        place = place_ref[k, 0]
        tile = stack[place, 0:lines, :].astype(jnp.float32)
        key_chain.append(stack[place, lines : lines + 8, 0:128].astype(jnp.float32)[0:1])
        normed = standardized(tile, gain).astype(jnp.bfloat16)
        if k == 0:
            asked = dot(normed, weights[0], BOTH_LAST).astype(jnp.bfloat16)
            put(query, asked.astype(jnp.float32))
            gate_ref[...] = dot(normed, weights[3], BOTH_LAST).astype(jnp.bfloat16)
        keys = dot(normed, weights[1], BOTH_LAST).astype(jnp.bfloat16)
        values = dot(normed, weights[2], BOTH_LAST).astype(jnp.bfloat16)
        for s in range(rows):
            part = slice(s * extent, (s + 1) * extent)
            key_rows[s, k * extent : (k + 1) * extent, :] = keys[part]
            value_ref[s, k * extent : (k + 1) * extent, :] = values[part]
    low = lax.broadcasted_iota(jnp.int32, (half, 128), 1) < extent
    head_lane = lane_block((half, width), FOCUS_BREADTH)
    is_open, chain = [], []
    for k in range(0, slots, 2):
        is_open.append(jnp.where(low, open_ref[k : k + 1, :], open_ref[k + 1 : k + 2, :]) > 0.0)
        chain.append(jnp.where(low[0:1], key_chain[k], key_chain[k + 1]))
    for p in range(2):
        same = [
            (chain_ref[p * half : (p + 1) * half, :] == one).astype(jnp.float32)
            for one in chain
        ]
        for s in range(rows):
            asked = take_every(query, s * extent + p, half, 2)
            asked = jnp.concatenate(
                [jnp.where(head_lane == h, asked, 0.0) for h in range(heads)], axis=0
            ).astype(jnp.bfloat16)
            scores = dot(asked, key_rows[s], BOTH_LAST) * FOCUS_BREADTH ** (-0.5)
            for h in range(heads):
                index = (group ^ (h // local_heads)) * local_heads + h % local_heads
                gain_row = chain_gain_ref[pl.ds(index, 1), :]
                rows_h = slice(h * half, (h + 1) * half)
                for q in range(slots // 2):
                    lanes = slice(q * 128, (q + 1) * 128)
                    score_ref[s, p, rows_h, lanes] = jnp.where(
                        is_open[q], scores[rows_h, lanes] + gain_row * same[q], MASKED
                    )


def attention(extent, rows, *refs):
    value_ref, gate_ref, score_ref, tile_ref = refs[:4]
    weight_refs, bias_refs = refs[4:8], refs[8:12]
    gain_ref = refs[12]
    row_ref, right_ref, pair, bias, attended = refs[13:]
    slots = pair.shape[0]
    heads = FOCUS_NUMBER
    local_heads = heads // 4
    width = row_ref.shape[1]
    half = extent // 2
    lines = rows * extent
    group = lax.axis_index("ch")
    for m in range(4):
        other = group ^ m
        pair[2 * lax.rem(other, 2) + other // 2] = bias_refs[m][...]

    low = lax.broadcasted_iota(jnp.int32, (half, 128), 1) < extent
    for k in range(0, slots, 2):
        lanes = slice((k // 2) * 128, (k // 2 + 1) * 128)
        for h in range(heads):
            rows_h = slice(h * half, (h + 1) * half)
            zero = pair[k, rows_h, :].astype(jnp.float32)
            one = pair[k + 1, rows_h, :].astype(jnp.float32)
            bias[0, rows_h, lanes] = jnp.where(low, zero, pltpu.roll(one, extent, 1))
            bias[1, rows_h, lanes] = jnp.where(low, pltpu.roll(zero, extent, 1), one)

    head_lane = lane_block((half, width), FOCUS_BREADTH)
    for s in range(rows):
        for p in range(2):
            parts = []
            for h in range(heads):
                index = (group ^ (h // local_heads)) * local_heads + h % local_heads
                start = pl.multiple_of(index * half, half)
                parts.append(
                    score_ref[s, p, h * half : (h + 1) * half, :]
                    + bias[p, pl.ds(start, half), :]
                )
            scores = jnp.concatenate(parts, axis=0)
            peak = jnp.max(scores, axis=1, keepdims=True)
            exponent = jnp.exp(scores - peak)
            share = 1.0 / jnp.sum(exponent, axis=1, keepdims=True)
            weight = (exponent * share).astype(jnp.bfloat16)
            mixed = dot(weight, value_ref[s], ACROSS)
            kept = jnp.zeros((half, width), jnp.float32)
            for h in range(heads):
                kept = kept + jnp.where(head_lane == h, mixed[h * half : (h + 1) * half], 0.0)
            put_every(attended, s * extent + p, 2, kept)
    gates = gate_ref[...].astype(jnp.float32)
    gated = (take(attended) * jax.nn.sigmoid(gates)).astype(jnp.bfloat16)
    out_weight = jnp.concatenate([ref[4] for ref in weight_refs], axis=0)
    change = dot(gated, out_weight, ACROSS)
    updated = (tile_ref[0:lines, :].astype(jnp.float32) + change).astype(jnp.bfloat16)
    row_ref[...] = updated
    opm = standardized(updated.astype(jnp.float32), gain_ref[...]).astype(jnp.bfloat16)
    factor = weight_refs[0][5].astype(jnp.float32)
    for ref in weight_refs[1:]:
        factor = factor + ref[5].astype(jnp.float32)
    factor = factor[0:PRODUCT_FEATURE].astype(jnp.bfloat16)
    right_ref[...] = dot(factor, opm, BOTH_LAST).astype(jnp.bfloat16)


def product_tables(*refs):
    piece_refs = refs[:4]
    table_ref, stack, turned, lined = refs[4:]
    features, narrow, channels = stack.shape[1:]
    share = channels // 4
    group = lax.axis_index("ch")
    deep = piece_refs[0].shape[1]
    for m in range(4):
        for i in range(features * narrow // deep):
            part = piece_refs[m][6 + i // 2, :, (i % 2) * 128 : (i % 2 + 1) * 128]
            few = deep // narrow
            stack[group ^ m, i * few : (i + 1) * few] = part.astype(
                jnp.float32
            ).reshape(few, narrow, channels)
    own = pl.multiple_of(group * share, share)
    lines = features // 4
    for block in range(lines):
        tall = jnp.concatenate(
            [
                stack[m, block * 4 + i]
                for i in range(4)
                for m in range(4)
            ],
            axis=0,
        )
        turned[...] = tall.T
        lined[pl.ds(block, share, stride=lines), :] = turned[pl.ds(own, share), :]
    lanes = lane_block((lines, 128), features)
    for z in range(share):
        rows = lined[z * lines : (z + 1) * lines, :]
        moved = [rows] + [pltpu.roll(rows, by * features, 1) for by in range(1, 4)]
        parts = [
            jnp.where(lanes == s, moved[(s - i) % 4], 0.0) for s in range(4) for i in range(4)
        ]
        table_ref[z // 2, :, (z % 2) * 128 : (z % 2 + 1) * 128] = jnp.concatenate(
            parts, axis=0
        ).astype(jnp.bfloat16)


def left_tables(extent, rows, *refs):
    piece_refs = refs[:4]
    factor_ref, gain_ref, weight_ref = refs[4:7]
    table_ref, result_ref = refs[7:9]
    spread, natural = refs[9:]
    half = extent // 2
    features = PRODUCT_FEATURE
    lines = rows * extent
    factor = jnp.concatenate([factor_ref[...]] * 4, axis=0)
    lanes = lane_block((lines, 128), features)
    left = jnp.zeros((lines, 128), jnp.float32)
    for m in range(4):
        piece = piece_refs[m][...]
        group = lax.axis_index("ch") ^ m
        for s in range(rows):
            result_ref[group * rows + s] = piece[s * extent : (s + 1) * extent]
        normed = standardized(piece.astype(jnp.float32), gain_ref[...]).astype(jnp.bfloat16)
        left = left + jnp.where(lanes == m, dot(normed, factor, BOTH_LAST), 0.0)
    natural[...] = left
    left = jnp.concatenate(
        [
            natural[pl.ds(s * extent + p, half, stride=2), :]
            for p in range(2)
            for s in range(rows)
        ],
        axis=0,
    ).astype(jnp.bfloat16)
    pairs = weight_ref.shape[0]
    for z in range(pairs):
        table = dot(left, weight_ref[z], ACROSS)
        for b in range(2 * rows):
            for q in range(2):
                spread[b, pl.ds(2 * z + q, half, stride=2 * pairs), :] = table[
                    b * half : (b + 1) * half, q * 128 : (q + 1) * 128
                ]
    for b in range(2 * rows):
        table_ref[:, b * 128 : (b + 1) * 128] = spread[b].astype(jnp.bfloat16)


def pick(place_ref, *refs):
    piece_refs = refs[:-2]
    out_ref, stack = refs[-2:]
    for m, ref in enumerate(piece_refs):
        stack[2 * m : 2 * m + 2] = ref[...]
    for k in range(out_ref.shape[0]):
        out_ref[k] = stack[place_ref[k, 0]]


def pair_update(extent, rows, scale, open_ref, table_ref, pair_ref, offset_ref, *refs):
    piece_refs = refs[:4]
    out_ref, right, held, sems = refs[4:]
    slots, channels, cells = pair_ref.shape
    low = lax.broadcasted_iota(jnp.int32, (4 * piece_refs[0].shape[1], 128), 1) < extent
    for k in range(slots):
        one = jnp.concatenate([ref[k] for ref in piece_refs], axis=0).astype(jnp.float32)
        turned = pltpu.roll(one, extent, 1)
        depth = one.shape[0]
        for p in range(2):
            for s in range(rows):
                value = one if s == p else turned
                value = jnp.where(low if p == 0 else jnp.logical_not(low), value, 0.0)
                start = (p * rows + s) * depth
                right[start : start + depth, k * 128 : (k + 1) * 128] = value.astype(
                    jnp.bfloat16
                )
    offset = offset_ref[...]
    keep = [open_ref[k : k + 1, :] for k in range(slots)]
    steps = sems.shape[0]
    stretch = cells // steps
    deep = stretch // 128
    copies = []
    for i in range(steps):
        total = dot(
            table_ref[i * deep * channels : (i + 1) * deep * channels, :], right[...], ACROSS
        )
        for k in range(slots):
            for line in range(deep):
                update = total[line * channels : (line + 1) * channels, k * 128 : (k + 1) * 128]
                update = update * scale + offset
                cell = slice((i * deep + line) * 128, (i * deep + line + 1) * 128)
                held[k, :, cell] = (
                    pair_ref[k, :, cell].astype(jnp.float32) + keep[k] * update
                ).astype(jnp.bfloat16)
        part = pl.ds(i * stretch, stretch)
        copies.append(
            pltpu.make_async_copy(held.at[:, :, part], out_ref.at[:, :, part], sems.at[i])
        )
        copies[-1].start()
    for copy in copies:
        copy.wait()


def on_device_small(*arguments):
    return small(*arguments)


def small(
    sequence_matrix,
    couple_matrix,
    block_target_entry,
    block_present_flag,
    amino_strand,
    sequence_scaling_factor,
    query_key_value_matrix,
    focus_result_matrix,
    strand_focus_offset,
    couple_scaling_factor,
    focus_offset_matrix,
    product_scaling_factor,
    first_factor_matrix,
    second_factor_matrix,
    product_result_matrix,
    product_result_offset,
):
    groups = lax.axis_size("ch")
    tiles = lax.axis_size("res")
    sequences, extent, width = sequence_matrix.shape
    slots, channels, cells = couple_matrix.shape
    rows = sequences // groups
    lines = rows * extent
    heads = FOCUS_NUMBER
    features = PRODUCT_FEATURE
    half = extent // 2
    inner = query_key_value_matrix.shape[2]
    block = width // 128

    def vmem(*shape):
        return pltpu.VMEM(shape, jnp.float32)

    def short(*shape):
        return jax.ShapeDtypeStruct(shape, jnp.bfloat16)

    def full(*shape):
        return jax.ShapeDtypeStruct(shape, jnp.float32)

    def in_hbm(values):
        return pltpu.with_memory_space_constraint(values, pltpu.HBM)

    second_rows = second_factor_matrix.T
    first_rows = first_factor_matrix.T
    product_rows = product_result_matrix.transpose(1, 2, 0).reshape(-1, C_Z)
    (
        tile_piece,
        weight_piece,
        pair_field,
        sum_weights,
        gain_one,
        gain_two,
        first_rows,
        offset,
        chain_column,
        chain_gain,
        place,
        present,
    ) = call(
        functools.partial(prepare, extent, rows),
        (
            short(lines + 8, width),
            short(6 + product_rows.size // (inner * width), inner, width),
            short(slots, channels, cells),
            short(4 * heads, channels),
            full(1, width),
            full(1, width),
            short(features, width),
            full(channels, 128),
            full(extent, 128),
            full(heads, 128),
            jax.ShapeDtypeStruct((slots, 128), jnp.int32),
            full(slots, 128),
        ),
        jax.tree.map(
            in_hbm,
            (
            sequence_matrix,
            couple_matrix,
            query_key_value_matrix.transpose(0, 2, 1),
            focus_result_matrix,
            second_rows,
            amino_strand.reshape(1, extent),
            couple_scaling_factor.reshape(1, channels),
            focus_offset_matrix.T,
            sequence_scaling_factor.reshape(1, width),
            product_scaling_factor.reshape(1, width),
            first_rows,
            product_result_offset.reshape(1, channels),
            strand_focus_offset.reshape(1, heads),
            product_rows,
            block_target_entry,
            block_present_flag,
            ),
        ),
        [pl.BlockSpec(memory_space=pltpu.HBM)] * 16,
        [
            pltpu.VMEM(second_rows.shape, jnp.bfloat16),
            pltpu.VMEM((1, extent), jnp.int32),
            vmem(1, channels),
            vmem(heads, channels),
            pltpu.VMEM((features, width), jnp.bfloat16),
            vmem(1, channels),
            vmem(1, heads),
            pltpu.SMEM((1, slots), jnp.int32),
            pltpu.SMEM((1, slots), jnp.int32),
            vmem(block, features, 128),
            vmem(extent, 128),
            pltpu.SemaphoreType.DMA((14 + rows + product_rows.shape[0] // inner,)),
        ],
        1_000_000,
        3_000_000,
    )

    weight_pieces = over_groups(weight_piece, True)

    tile_pieces = over_tiles(tile_piece)

    sums_shape = (slots // 2, heads, cells + cells // (heads // 2) + 128)

    def sums_of(keep):
        return call(
            functools.partial(pair_sums, keep),
            jax.ShapeDtypeStruct(sums_shape, jnp.float32),
            (sum_weights, pair_field),
            [spec()] * 2,
            [],
            2 * slots // 2 * cells * channels * 4 * heads,
            couple_matrix.size,
        )

    given = sums_of(False)
    taken = flip(given, "ch", 1)
    kept = sums_of(True)
    merged, sent = call(
        functools.partial(merge_sums, channels),
        (full(*sums_shape[1:]), full(*sums_shape[1:])),
        (kept, taken),
        [spec()] * 2,
        [],
        given.size * 4,
        given.size * 12,
    )
    far_sums = flip(sent, "ch", 2)
    own_bias = call(
        functools.partial(pair_bias, extent),
        short(heads * half, 128),
        (merged, far_sums),
        [spec()] * 2,
        [vmem(heads * half, 128)],
        given.size * 4,
        given.size * 8,
    )
    bias_pieces = over_groups(own_bias, True)

    own_weights = call(
        product_tables,
        short(channels // 2, 128, 256),
        tuple(weight_pieces),
        [spec()] * 4,
        [
            vmem(groups, features, features // groups, C_Z),
            vmem(C_Z, 128),
            vmem(channels * features // 4, 128),
        ],
        1_000_000,
        2_000_000,
    )

    values, gates, scores = call(
        functools.partial(project, extent, rows, tiles),
        (
            short(rows, slots * extent, width),
            short(lines, width),
            full(rows, 2, heads * half, slots * extent),
        ),
        (
            place,
            *tile_pieces,
            *weight_pieces,
            gain_one,
            chain_column,
            chain_gain,
            present,
        ),
        [spec()] * (tiles + 9),
        [
            pltpu.VMEM((tiles, lines + 8, width), jnp.bfloat16),
            pltpu.VMEM((rows, slots * extent, width), jnp.bfloat16),
            vmem(block, lines, 128),
        ],
        200_000_000,
        2_000_000,
    )
    row_piece, right_piece = call(
        functools.partial(attention, extent, rows),
        (short(lines, width), short(features, lines)),
        (
            values,
            gates,
            scores,
            tile_piece,
            *weight_pieces,
            *bias_pieces,
            gain_two,
        ),
        [spec()] * 13,
        [
            pltpu.VMEM((slots, heads * half, 128), jnp.bfloat16),
            vmem(2, heads * half, slots * extent),
            vmem(block, lines, 128),
        ],
        600_000_000,
        3_000_000,
    )

    turned = flip(right_piece, "res", 1)
    stacked = jnp.stack([right_piece, turned])
    right_pieces = [stacked] + [flip(stacked, "res", bits) for bits in range(2, tiles, 2)]
    picked = call(
        pick,
        short(slots, features, lines),
        (place, *right_pieces),
        [spec()] * (1 + tiles // 2),
        [pltpu.VMEM((tiles, features, lines), jnp.bfloat16)],
        1000,
        200_000,
    )
    right_tiles = over_groups(picked, False)
    row_pieces = over_groups(row_piece, False)

    table, sequence_result_matrix = call(
        functools.partial(left_tables, extent, rows),
        (
            short(half * channels, 2 * rows * 128),
            short(sequences, extent, width),
        ),
        (*row_pieces, first_rows, gain_two, own_weights),
        [spec()] * 7,
        [vmem(2 * rows, half * channels, 128), vmem(lines, 128)],
        300_000_000,
        3_000_000,
    )

    steps = 8
    pairwise_output = pl.pallas_call(
        functools.partial(pair_update, extent, rows, 1.0 / sequences),
        out_shape=jax.ShapeDtypeStruct(couple_matrix.shape, jnp.bfloat16),
        in_specs=[spec()] * 8,
        out_specs=pl.BlockSpec(memory_space=pl.ANY),
        scratch_shapes=[
            pltpu.VMEM((table.shape[1], slots * 128), jnp.bfloat16),
            pltpu.VMEM(couple_matrix.shape, jnp.bfloat16),
            pltpu.SemaphoreType.DMA((steps,)),
        ],
        name="pair_update",
        cost_estimate=pl.CostEstimate(
            flops=600_000_000, bytes_accessed=3_000_000, transcendentals=0
        ),
        compiler_params=pltpu.CompilerParams(vmem_limit_bytes=VMEM_LIMIT),
    )(present, table, pair_field, offset, *right_tiles)
    return (sequence_result_matrix, pairwise_output)


def solution(mesh):
    few = mesh.shape["res"] <= 8 and mesh.shape["ch"] == 4
    return jax.shard_map(
        on_device_small if few else on_device,
        mesh=mesh,
        in_specs=(
            P(None, "res", None),
            P("res", "ch", None),
            P("res", None),
            P("res", None),
            P("res"),
            P(),
            P(None, None, "ch"),
            P("ch", None),
            P(),
            P("ch"),
            P("ch", None),
            P(),
            P(),
            P(None, "ch"),
            P(None, None, "ch"),
            P("ch"),
        ),
        out_specs=(P(None, "res", None), P("res", "ch", None)),
        check_vma=False,
    )
```
